256 devices in a mesh: feat: 4 (over y), rows: 64 (over x, z, core).
Axes of the slice: x: 4, y: 4, z: 8, core: 2. Of those that a mesh axis runs over, the one named last changes fastest.
Arguments:
- features: bfloat16 [16384, 4096], P('rows', 'feat'), may hold values from -16 to 16
- labels: int32 [16384], P('rows'), may hold values from 0 to 639
- inv_gram: float32 [4, 1024, 1024], P('feat'), may hold values from -1 to 1, as said below
Outputs:
- weights: float32 [4096, 640], P(('feat', 'rows'))
- after_block: float32 [4, 16384, 640], P('feat', 'rows')
The draws below stay inside these ranges and needn't reach their ends.
Inputs may be any that keep to these rules, and one draw needn't show every extreme that they name: Each of the 4 matrices of inv_gram is symmetric.
All inputs are finite; a program needn't handle non-finite values.
Results may differ from the reference program's by a relative error of at most 0.0094.
Values sent between devices are 32-bit elements; how exact they have to be, the bound alone decides.
No kernel may reach another device: no remote copies, remote signals or barrier semaphores. Data moves between devices by JAX's collectives and lax.ppermute only.
A program may use at most 64 MiB of HBM per device.

```python
import math
import jax
import jax.numpy as jnp
from jax import lax

BW = 1024
C = 640
ROW_DEV = 256
NBLK = 4
ROWS = 16384


def draw_labels(key, part):
    keys = jax.random.split(jax.random.fold_in(key, 11), 4)
    half = C // 2
    narrow_span = max(half // 4, 1)
    shard_total = ROWS // ROW_DEV
    positions = jnp.arange(ROWS, dtype=jnp.int32)
    shard_ids = positions // ROW_DEV
    first_half = jax.random.randint(keys[0], (ROWS,), 0, 3 * shard_total) < shard_total + 2 * shard_ids
    narrow = jax.random.randint(keys[1], (ROWS,), 0, 2) == 0
    wide_ids = jax.random.randint(keys[2], (ROWS,), 0, half)
    narrow_ids = jax.random.randint(keys[3], (ROWS,), 0, narrow_span)
    within = jnp.where(narrow, narrow_ids, wide_ids)
    return jnp.where(first_half, within, half + within).astype(jnp.int32)


def draw_inv_gram(key, part):
    keys = jax.random.split(jax.random.fold_in(key, 23), 2)
    low_end, high_end = (0.5, 2.0)
    diag_values = jnp.exp(jax.random.uniform(keys[0], (NBLK, BW), jnp.float32, math.log(low_end), math.log(high_end)))
    noise = jax.random.normal(keys[1], (NBLK, BW, BW), jnp.float32) * (0.2 / math.sqrt(BW))
    symmetric = (noise + jnp.transpose(noise, (0, 2, 1))) / math.sqrt(2.0)
    identity = jnp.eye(BW, dtype=jnp.float32)
    return (0.25 / BW * (symmetric + diag_values[:, :, None] * identity[None, :, :])).astype(jnp.float32)


def strengthened(values, key, source, target, parts, factor):
    def block_of(axis_at):
        return (jnp.arange(values.shape[axis_at]) // (values.shape[axis_at] // parts)).reshape((-1,) + (1,) * (values.ndim - 1 - axis_at))

    one_side = jax.random.permutation(key, parts)[block_of(target)]
    second = (block_of(target) + parts // 2) % parts
    return jnp.where((block_of(source) == one_side) | (block_of(source) == second), factor * values, values)


def shard_levels(key, extent, cuts, low, top_value):
    loudness = 1.0
    for dim, blocks in cuts:
        heights = jax.random.uniform(jax.random.fold_in(jax.random.fold_in(key, 6), dim), (blocks,), jnp.float32, low / len(cuts), top_value / len(cuts))
        loudness = loudness * jnp.repeat(jnp.exp(heights), extent[dim] // blocks).reshape((-1,) + (1,) * (len(extent) - 1 - dim))
    return loudness


def noise_with(key, extent, scale, reach, pieces, heavy, kind=jnp.bfloat16):
    drawn = scale * jax.random.normal(key, extent, jnp.float32)
    if pieces:
        drawn = drawn * shard_levels(key, extent, pieces, -0.22, 0.18)
    return jnp.clip(strengthened(drawn, jax.random.fold_in(key, 3), *heavy), -reach, reach).astype(kind)


def setup_inputs(seed: int = 0) -> dict:
    arg_keys = jax.random.split(jax.random.key(seed), 4)
    features = noise_with(arg_keys[0], (ROWS, NBLK * BW), 1.0, 16.0, ((0, 64), (1, 4)), (0, 1, 64, 4.0))
    labels = draw_labels(jax.random.fold_in(arg_keys[3], 71), 0)
    inv_gram = draw_inv_gram(jax.random.fold_in(arg_keys[3], 71), 0)
    return {"features": features, "labels": labels, "inv_gram": inv_gram}


def reference(features, labels, inv_gram):
    total_rows = labels.shape[0]
    counts = jnp.zeros((C,), jnp.float32).at[labels].add(1.0)
    row_weight = total_rows / (C * counts[labels])
    class_ids = jnp.arange(C, dtype=jnp.int32)
    residual = (labels[:, None] == class_ids[None, :]).astype(jnp.float32)
    weight_list = []
    residual_list = []
    for index in range(NBLK):
        feature_block = features[:, index * BW:(index + 1) * BW]
        scaled = (row_weight[:, None] * residual).astype(jnp.bfloat16)
        partial_value = lax.dot_general(feature_block, scaled, (((0,), (0,)), ((), ())), preferred_element_type=jnp.float32)
        solved = jnp.dot(inv_gram[index], partial_value, precision=lax.Precision.HIGHEST, preferred_element_type=jnp.float32)
        residual = residual - jnp.dot(feature_block, solved.astype(jnp.bfloat16), preferred_element_type=jnp.float32)
        weight_list.append(solved)
        residual_list.append(residual)
    return jnp.concatenate(weight_list, axis=0), jnp.stack(residual_list, axis=0)
```

```python
import functools

import jax
import jax.numpy as jnp
from jax import lax
from jax.experimental import pallas as pl
from jax.experimental.pallas import tpu as pltpu
from jax.sharding import Mesh, PartitionSpec as P

C = 640
LANES = 128
XZ = ("x", "z")
F32 = jnp.float32
BF16 = jnp.bfloat16
VMEM = pl.BlockSpec(memory_space=pltpu.VMEM)
SMEM = pl.BlockSpec(memory_space=pltpu.SMEM)


def dot(left, right):
    return jnp.dot(left, right, preferred_element_type=F32)


def dot_t(left, right):
    return lax.dot_general(left, right, (((1,), (1,)), ((), ())), preferred_element_type=F32)


def swap_cores(value):
    return lax.ppermute(value, "core", [(0, 1), (1, 0)])


def prepare_kernel(gram_ref, x_ref, zt_ref, xf_ref):
    gram = gram_ref[0]
    high = gram.astype(BF16)
    rest = gram - high.astype(F32)
    mid = rest.astype(BF16)
    low = (rest - mid.astype(F32)).astype(BF16)
    x = x_ref[...]
    zt_ref[...] = (dot_t(low, x) + dot_t(mid, x)) + dot_t(high, x)

    @pl.when(pl.program_id(0) == 0)
    def _():
        xf_ref[...] = x.astype(F32)


def prepare(features, inv_gram, tile=256):
    rows, width = features.shape
    return pl.pallas_call(
        prepare_kernel,
        grid=(width // tile,),
        in_specs=[
            pl.BlockSpec((1, tile, width), lambda i: (0, i, 0)),
            pl.BlockSpec((rows, width), lambda i: (0, 0)),
        ],
        out_specs=[
            pl.BlockSpec((tile, rows), lambda i: (i, 0)),
            pl.BlockSpec((rows, width), lambda i: (0, 0)),
        ],
        out_shape=[
            jax.ShapeDtypeStruct((width, rows), F32),
            jax.ShapeDtypeStruct((rows, width), F32),
        ],
    )(inv_gram, features)


def partial_sum(zt_refs, scaled_halves):
    total = None
    for zt_ref, scaled in zip(zt_refs, scaled_halves):
        zt = zt_ref[0]
        high = zt.astype(BF16)
        low = (zt - high.astype(F32)).astype(BF16)
        part = dot(low, scaled) + dot(high, scaled)
        total = part if total is None else total + part
    return total


def label_parts(lab, slices, width):
    group = jnp.zeros_like(lab)
    for d in range(1, slices):
        group = group + (lab >= d * width).astype(jnp.int32)
    return group, lab - group * width


def first_kernel(slices, slice_ref, lab_ref, labt_ref, za_ref, zb_ref, out_ref):
    width = C // slices
    lab = lab_ref[...]
    rows = lab.shape[0] // 2
    group, low_label = label_parts(lab, slices, width)
    lane = lax.broadcasted_iota(jnp.int32, (lab.shape[0], LANES), 1)
    low_hot = jnp.where(low_label == lane, 1.0, 0.0)
    onehot = jnp.where(group == slice_ref[0], low_hot, 0.0).astype(BF16)
    labt = labt_ref[...]
    first = lax.broadcasted_iota(jnp.int32, (slices, labt.shape[1]), 0) * width
    group_hot = jnp.where((labt >= first) & (labt < first + width), 1.0, 0.0).astype(BF16)
    counts = dot(group_hot, low_hot.astype(BF16))
    total = partial_sum((za_ref, zb_ref), (onehot[:rows], onehot[rows:]))
    chips, deep, _ = out_ref.shape
    out_ref[:, : deep - slices, :] = total.reshape(chips, deep - slices, LANES)
    out_ref[:, deep - slices :, :] = jnp.broadcast_to(counts[None], (chips, slices, LANES))


def middle_kernel(slices, total_rows, slice_ref, in_ref, *out_refs):
    summed = jnp.sum(in_ref[...], axis=0)
    solved_ref, copies_ref = out_refs[0], out_refs[1]
    chunk = solved_ref.shape[0]
    solved = summed[:chunk]
    if len(out_refs) == 3:
        totals = summed[chunk:]
        out_refs[2][...] = totals
        row = lax.broadcasted_iota(jnp.int32, totals.shape, 0)
        mine = jnp.sum(jnp.where(row == slice_ref[0], totals, 0.0), axis=0, keepdims=True)
        scale = jnp.where(mine > 0.0, total_rows / (C * jnp.maximum(mine, 1.0)), 0.0)
        solved = solved * scale.astype(BF16).astype(F32)
    solved_ref[...] = solved
    copies_ref[...] = jnp.broadcast_to(solved[None], copies_ref.shape)


def middle(slices, total_rows, slice_index, arrived, chunk):
    chips, deep, _ = arrived.shape
    shapes = [
        jax.ShapeDtypeStruct((chunk, LANES), F32),
        jax.ShapeDtypeStruct((chips, chunk, LANES), F32),
    ]
    if deep > chunk:
        shapes.append(jax.ShapeDtypeStruct((slices, LANES), F32))
    return pl.pallas_call(
        functools.partial(middle_kernel, slices, total_rows),
        in_specs=[SMEM, VMEM],
        out_specs=[VMEM] * len(shapes),
        out_shape=shapes,
    )(slice_index, arrived)


def update(everyone_ref, xa_ref, xb_ref, residual):
    solved = everyone_ref[...].reshape(-1, LANES).astype(BF16)
    rows = xa_ref.shape[1]
    halves = (
        residual[:rows] - dot(xa_ref[0].astype(BF16), solved),
        residual[rows:] - dot(xb_ref[0].astype(BF16), solved),
    )
    return halves


def second_kernel(
    slices, total_rows, slice_ref, lab_ref, totals_ref, everyone_ref, xa_ref, xb_ref,
    za_ref, zb_ref, residual_ref, weight_ref, out_ref,
):
    width = C // slices
    lab = lab_ref[...]
    group, low_label = label_parts(lab, slices, width)
    lane = lax.broadcasted_iota(jnp.int32, (lab.shape[0], LANES), 1)
    hit = low_label == lane
    spread = jnp.zeros((lab.shape[0], LANES), F32)
    for d in range(slices):
        spread = jnp.where(group == d, totals_ref[d : d + 1, :], spread)
    row_count = jnp.sum(jnp.where(hit, spread, 0.0), axis=1, keepdims=True)
    weight = total_rows / (C * row_count)
    weight_ref[...] = jnp.broadcast_to(weight, weight_ref.shape)
    onehot = jnp.where(hit & (group == slice_ref[0]), 1.0, 0.0)
    halves = update(everyone_ref, xa_ref, xb_ref, onehot)
    rows = xa_ref.shape[1]
    residual_ref[:rows] = halves[0]
    residual_ref[rows:] = halves[1]
    scaled = [
        (weight[k * rows : (k + 1) * rows] * halves[k]).astype(BF16) for k in range(2)
    ]
    total = partial_sum((za_ref, zb_ref), scaled)
    out_ref[...] = total.reshape(out_ref.shape)


def step_kernel(
    everyone_ref, xa_ref, xb_ref, za_ref, zb_ref, old_ref, weight_ref, residual_ref, out_ref
):
    halves = update(everyone_ref, xa_ref, xb_ref, old_ref[...])
    rows = xa_ref.shape[1]
    residual_ref[:rows] = halves[0]
    residual_ref[rows:] = halves[1]
    scaled = [
        (weight_ref[k * rows : (k + 1) * rows] * halves[k]).astype(BF16) for k in range(2)
    ]
    total = partial_sum((za_ref, zb_ref), scaled)
    out_ref[...] = total.reshape(out_ref.shape)


def last_kernel(everyone_ref, xa_ref, xb_ref, old_ref, residual_ref):
    halves = update(everyone_ref, xa_ref, xb_ref, old_ref[...])
    rows = xa_ref.shape[1]
    residual_ref[:rows] = halves[0]
    residual_ref[rows:] = halves[1]


def join_kernel(in_ref, weights_ref, after_ref):
    slices = in_ref.shape[0]
    width = C // slices
    head = weights_ref.shape[0]
    for d in range(slices):
        weights_ref[:, d * width : (d + 1) * width] = in_ref[d, :head, :width]
        after_ref[0, :, d * width : (d + 1) * width] = in_ref[d, head:, :width]


def local(features, labels, inv_gram):
    rows_here, block_width = features.shape
    blocks = lax.axis_size("feat")
    cores = lax.axis_size("core")
    chips = lax.axis_size("x") * lax.axis_size("z")
    slices = blocks * cores
    chunk = block_width // chips
    core = lax.axis_index("core")
    slice_index = (lax.axis_index("feat") * cores + core).astype(jnp.int32)[None]
    total_rows = float(rows_here * chips * cores)
    both = cores * rows_here

    zt_own, x_own = prepare(features, inv_gram)
    zt_mine = lax.all_gather(zt_own, "feat")
    x_mine = lax.all_gather(x_own, "feat")
    zt_other = swap_cores(zt_mine)
    x_other = swap_cores(x_mine)
    lab = jnp.concatenate([labels, swap_cores(labels)])
    lab_column, lab_row = lab[:, None], lab[None, :]

    def z_spec(b):
        return pl.BlockSpec((1, block_width, rows_here), lambda i: (b, 0, 0))

    def x_spec(b):
        return pl.BlockSpec((1, rows_here, block_width), lambda i: (b, 0, 0))

    def whole(*shape):
        return pl.BlockSpec(shape, lambda i: (0,) * len(shape))

    pieces_shape = jax.ShapeDtypeStruct((chips, chunk, LANES), F32)
    rows_shape = jax.ShapeDtypeStruct((both, LANES), F32)
    rows_block = whole(both, LANES)
    pieces_block = whole(chips, chunk, LANES)

    pieces = pl.pallas_call(
        functools.partial(first_kernel, slices),
        grid=(1,),
        in_specs=[SMEM, whole(both, 1), whole(1, both), z_spec(0), z_spec(0)],
        out_specs=whole(chips, chunk + slices, LANES),
        out_shape=jax.ShapeDtypeStruct((chips, chunk + slices, LANES), F32),
    )(slice_index, lab_column, lab_row, zt_mine, zt_other)

    kept_rows = []
    kept_solved = []
    totals = weight = residual = None
    for b in range(blocks):
        arrived = lax.all_to_all(pieces, XZ, 0, 0, tiled=True)
        result = middle(slices, total_rows, slice_index, arrived, chunk)
        kept_solved.append(result[0])
        if b == 0:
            totals = result[2]
        everyone = lax.all_to_all(result[1], XZ, 0, 0, tiled=True)
        if b == 0:
            residual, weight, pieces = pl.pallas_call(
                functools.partial(second_kernel, slices, total_rows),
                grid=(1,),
                in_specs=[SMEM, whole(both, 1), whole(slices, LANES), pieces_block,
                          x_spec(b), x_spec(b), z_spec(b + 1), z_spec(b + 1)],
                out_specs=[rows_block, rows_block, pieces_block],
                out_shape=[rows_shape, rows_shape, pieces_shape],
            )(slice_index, lab_column, totals, everyone, x_mine, x_other, zt_mine, zt_other)
        elif b < blocks - 1:
            residual, pieces = pl.pallas_call(
                step_kernel,
                grid=(1,),
                in_specs=[pieces_block, x_spec(b), x_spec(b), z_spec(b + 1), z_spec(b + 1),
                          rows_block, rows_block],
                out_specs=[rows_block, pieces_block],
                out_shape=[rows_shape, pieces_shape],
            )(everyone, x_mine, x_other, zt_mine, zt_other, residual, weight)
        else:
            residual = pl.pallas_call(
                last_kernel,
                grid=(1,),
                in_specs=[pieces_block, x_spec(b), x_spec(b), rows_block],
                out_specs=rows_block,
                out_shape=rows_shape,
            )(everyone, x_mine, x_other, residual)
        kept_rows.append(residual)

    half = chunk // cores
    sends = []
    for b in range(blocks):
        own = kept_rows[b][:rows_here]
        other = kept_rows[b][rows_here:]
        for k in range(cores):
            sends.append(kept_solved[b][k * half:(k + 1) * half])
            sends.append(jnp.where(core == k, own, other))
    sends = jnp.concatenate(sends, axis=0).reshape(slices, half + rows_here, LANES)
    got = lax.all_to_all(sends, ("feat", "core"), 0, 0, tiled=True)
    return pl.pallas_call(
        join_kernel,
        in_specs=[VMEM],
        out_specs=[VMEM, VMEM],
        out_shape=[
            jax.ShapeDtypeStruct((half, C), F32),
            jax.ShapeDtypeStruct((1, rows_here, C), F32),
        ],
    )(got)


def solution(mesh):
    sizes = dict(mesh.shape)
    fine = Mesh(mesh.devices.reshape(sizes["feat"], 4, 8, 2), ("feat", "x", "z", "core"))
    rows = ("x", "z", "core")
    in_specs = (P(rows, "feat"), P(rows), P("feat", None, None))
    out_specs = (P(("feat",) + rows, None), P("feat", rows, None))
    return jax.shard_map(local, mesh=fine, in_specs=in_specs, out_specs=out_specs, check_vma=False)
```

```python
import functools

import jax
import jax.numpy as jnp
from jax import lax
from jax.experimental import pallas as pl
from jax.experimental.pallas import tpu as pltpu
from jax.sharding import Mesh, PartitionSpec as P

C = 640
LANES = 128
XZ = ("x", "z")
F32 = jnp.float32
BF16 = jnp.bfloat16
VMEM = pl.BlockSpec(memory_space=pltpu.VMEM)
SMEM = pl.BlockSpec(memory_space=pltpu.SMEM)


def room(mib):
    return pltpu.CompilerParams(vmem_limit_bytes=mib << 20)


def dot(left, right):
    return jnp.dot(left, right, preferred_element_type=F32)


def dot_t(left, right):
    return lax.dot_general(left, right, (((1,), (1,)), ((), ())), preferred_element_type=F32)


def swap_cores(value):
    return lax.ppermute(value, "core", [(0, 1), (1, 0)])


def prepare_kernel(gram_ref, x_ref, z0_ref, z1_ref, x0_ref, x1_ref):
    step = pl.program_id(0)
    gram = gram_ref[0]
    high = gram.astype(BF16)
    rest = gram - high.astype(F32)
    mid = rest.astype(BF16)
    low = (rest - mid.astype(F32)).astype(BF16)
    x = x_ref[...]
    zt = (dot_t(low, x) + dot_t(mid, x)) + dot_t(high, x)
    tile = zt.shape[0]
    per_half = z0_ref.shape[0] // tile

    @pl.when(step < per_half)
    def _():
        z0_ref[pl.ds(pl.multiple_of(step * tile, tile), tile), :] = zt

    @pl.when(step >= per_half)
    def _():
        z1_ref[pl.ds(pl.multiple_of((step - per_half) * tile, tile), tile), :] = zt

    @pl.when(step == 0)
    def _():
        half = x0_ref.shape[0]
        x0_ref[...] = x[:half].astype(F32)
        x1_ref[...] = x[half:].astype(F32)


def prepare(features, inv_gram, tile=256):
    rows, width = features.shape
    z_shape = (width // 2, rows)
    x_shape = (rows // 2, width)
    return pl.pallas_call(
        prepare_kernel,
        grid=(width // tile,),
        in_specs=[
            pl.BlockSpec((1, tile, width), lambda i: (0, i, 0)),
            pl.BlockSpec((rows, width), lambda i: (0, 0)),
        ],
        out_specs=[pl.BlockSpec(z_shape, lambda i: (0, 0))] * 2
        + [pl.BlockSpec(x_shape, lambda i: (0, 0))] * 2,
        out_shape=[jax.ShapeDtypeStruct(z_shape, F32)] * 2
        + [jax.ShapeDtypeStruct(x_shape, F32)] * 2,
        compiler_params=room(24),
    )(inv_gram, features)


def held(shape, dtype=F32):
    return pltpu.VMEM(shape, dtype)


def near(value):
    return pltpu.with_memory_space_constraint(value, pltpu.VMEM)


def fetch(slot_ref, refs, landing, sems):
    for slot in range(len(refs) // 4):

        @pl.when(slot_ref[0] == slot)
        def _():
            for q in range(4):
                pltpu.make_async_copy(refs[slot * 4 + q], landing.at[q], sems.at[q]).start()

    for q in range(4):
        pltpu.make_async_copy(refs[q], landing.at[q], sems.at[q]).wait()


def gather_z_kernel(slot_ref, *refs):
    high_ref, low_ref, landing, sems = refs[-4:]
    fetch(slot_ref, refs[:-4], landing, sems)
    half_rows = high_ref.shape[0] // 2
    half_cols = high_ref.shape[1] // 2
    for k in range(2):
        for h in range(2):
            value = landing[k * 2 + h]
            high = value.astype(BF16)
            rows = pl.ds(h * half_rows, half_rows)
            cols = pl.ds(k * half_cols, half_cols)
            high_ref[rows, cols] = high
            low_ref[rows, cols] = (value - high.astype(F32)).astype(BF16)


def gather_x_kernel(slot_ref, *refs):
    out_ref, landing, sems = refs[-3:]
    fetch(slot_ref, refs[:-3], landing, sems)
    piece = out_ref.shape[0] // 4
    for q in range(4):
        out_ref[pl.ds(q * piece, piece), :] = landing[q].astype(BF16)


def gather(kernel, outs, slot, quarters):
    return pl.pallas_call(
        kernel,
        in_specs=[SMEM] + [pl.BlockSpec(memory_space=pl.ANY)] * len(quarters),
        out_specs=[VMEM] * len(outs),
        out_shape=[held(shape, BF16) for shape in outs],
        scratch_shapes=[
            pltpu.VMEM((4,) + quarters[0].shape, F32),
            pltpu.SemaphoreType.DMA((4,)),
        ],
        compiler_params=room(12),
        cost_estimate=pl.CostEstimate(flops=0, bytes_accessed=6 << 20, transcendentals=0),
    )(slot, *quarters)


def partial_sum(high_ref, low_ref, scaled):
    return dot(low_ref[...], scaled) + dot(high_ref[...], scaled)


def label_parts(lab, slices, width):
    group = jnp.zeros_like(lab)
    for d in range(1, slices):
        group = group + (lab >= d * width).astype(jnp.int32)
    return group, lab - group * width


def first_kernel(slices, slice_ref, lab_ref, labt_ref, high_ref, low_ref, out_ref):
    width = C // slices
    lab = lab_ref[...]
    group, low_label = label_parts(lab, slices, width)
    lane = lax.broadcasted_iota(jnp.int32, (lab.shape[0], LANES), 1)
    low_hot = jnp.where(low_label == lane, 1.0, 0.0)
    onehot = jnp.where(group == slice_ref[0], low_hot, 0.0).astype(BF16)
    labt = labt_ref[...]
    first = lax.broadcasted_iota(jnp.int32, (slices, labt.shape[1]), 0) * width
    group_hot = jnp.where((labt >= first) & (labt < first + width), 1.0, 0.0).astype(BF16)
    counts = dot(group_hot, low_hot.astype(BF16))
    total = partial_sum(high_ref, low_ref, onehot)
    chips, deep, _ = out_ref.shape
    out_ref[:, : deep - slices, :] = total.reshape(chips, deep - slices, LANES)
    out_ref[:, deep - slices :, :] = jnp.broadcast_to(counts[None], (chips, slices, LANES))


def middle_kernel(slices, total_rows, slice_ref, in_ref, *out_refs):
    summed = jnp.sum(in_ref[...], axis=0)
    solved_ref, copies_ref = out_refs[0], out_refs[1]
    chunk = solved_ref.shape[0]
    solved = summed[:chunk]
    if len(out_refs) == 3:
        totals = summed[chunk:]
        out_refs[2][...] = totals
        row = lax.broadcasted_iota(jnp.int32, totals.shape, 0)
        mine = jnp.sum(jnp.where(row == slice_ref[0], totals, 0.0), axis=0, keepdims=True)
        scale = jnp.where(mine > 0.0, total_rows / (C * jnp.maximum(mine, 1.0)), 0.0)
        solved = solved * scale.astype(BF16).astype(F32)
    solved_ref[...] = solved
    copies_ref[...] = jnp.broadcast_to(solved[None], copies_ref.shape)


def middle(slices, total_rows, slice_index, arrived, chunk):
    chips, deep, _ = arrived.shape
    shapes = [held((chunk, LANES)), held((chips, chunk, LANES))]
    if deep > chunk:
        shapes.append(held((slices, LANES)))
    return pl.pallas_call(
        functools.partial(middle_kernel, slices, total_rows),
        in_specs=[SMEM, VMEM],
        out_specs=[VMEM] * len(shapes),
        out_shape=shapes,
        compiler_params=room(8),
    )(slice_index, near(arrived))


def update(everyone_ref, x_ref, residual):
    solved = everyone_ref[...].reshape(-1, LANES).astype(BF16)
    return residual - dot(x_ref[...], solved)


def second_kernel(
    slices, total_rows, slice_ref, lab_ref, totals_ref, everyone_ref, x_ref, high_ref,
    low_ref, residual_ref, weight_ref, out_ref,
):
    width = C // slices
    lab = lab_ref[...]
    group, low_label = label_parts(lab, slices, width)
    lane = lax.broadcasted_iota(jnp.int32, (lab.shape[0], LANES), 1)
    hit = low_label == lane
    spread = jnp.zeros((lab.shape[0], LANES), F32)
    for d in range(slices):
        spread = jnp.where(group == d, totals_ref[d : d + 1, :], spread)
    row_count = jnp.sum(jnp.where(hit, spread, 0.0), axis=1, keepdims=True)
    weight = total_rows / (C * row_count)
    weight_ref[...] = jnp.broadcast_to(weight, weight_ref.shape)
    onehot = jnp.where(hit & (group == slice_ref[0]), 1.0, 0.0)
    residual = update(everyone_ref, x_ref, onehot)
    residual_ref[...] = residual
    total = partial_sum(high_ref, low_ref, (weight * residual).astype(BF16))
    out_ref[...] = total.reshape(out_ref.shape)


def step_kernel(
    everyone_ref, x_ref, high_ref, low_ref, old_ref, weight_ref, residual_ref, out_ref
):
    residual = update(everyone_ref, x_ref, old_ref[...])
    residual_ref[...] = residual
    total = partial_sum(high_ref, low_ref, (weight_ref[...] * residual).astype(BF16))
    out_ref[...] = total.reshape(out_ref.shape)


def last_kernel(blocks, core_ref, everyone_ref, x_ref, *refs):
    solved_refs, rows_refs, out_ref = refs[:blocks], refs[blocks:-1], refs[-1]
    rows = rows_refs[0].shape[0] // 2
    half = solved_refs[0].shape[0] // 2
    last = update(everyone_ref, x_ref, rows_refs[-1][...])
    for b in range(blocks):
        for k in range(2):
            out_ref[2 * b + k, :half] = solved_refs[b][k * half : (k + 1) * half]
            if b < blocks - 1:
                begin = jnp.where(core_ref[0] == k, 0, rows)
                begin = pl.multiple_of(begin, rows)
                out_ref[2 * b + k, half:] = rows_refs[b][pl.ds(begin, rows), :]
            else:
                mine = jnp.where(core_ref[0] == k, last[:rows], last[rows:])
                out_ref[2 * b + k, half:] = mine


def join_kernel(in_ref, weights_ref, after_ref):
    slices = in_ref.shape[0]
    width = C // slices
    head = weights_ref.shape[0]
    for d in range(slices):
        weights_ref[:, d * width : (d + 1) * width] = in_ref[d, :head, :width]
        after_ref[0, :, d * width : (d + 1) * width] = in_ref[d, head:, :width]


def shifted(value, by):
    count = lax.axis_size("feat")
    return lax.ppermute(value, "feat", [(i, (i + by) % count) for i in range(count)])


def all_slots(own, forward=None):
    up0, down1, up1, down0 = (
        shifted(own[0], 1), shifted(own[1], -1), shifted(own[1], 1), shifted(own[0], -1)
    )
    if forward is not None:
        up0, down1, up1, down0 = forward(up0, down1, up1, down0)
    far0, far1 = shifted(up0, 1), shifted(down1, -1)
    slots = [own, (up0, up1), (far0, far1), (down0, down1)]
    return slots, (up1, down0)


def with_other_core(slots):
    quarters = []
    for halves in slots:
        quarters += [halves[0], halves[1], swap_cores(halves[0]), swap_cores(halves[1])]
    return quarters


def local(features, labels, inv_gram):
    rows_here, block_width = features.shape
    blocks = lax.axis_size("feat")
    cores = lax.axis_size("core")
    chips = lax.axis_size("x") * lax.axis_size("z")
    slices = blocks * cores
    chunk = block_width // chips
    core = lax.axis_index("core").astype(jnp.int32)
    feat = lax.axis_index("feat").astype(jnp.int32)
    core_index = core[None]
    slice_index = (feat * cores + core)[None]
    total_rows = float(rows_here * chips * cores)
    both = cores * rows_here

    lab = jnp.concatenate([labels, swap_cores(labels)])
    lab_column, lab_row = lab[:, None], lab[None, :]
    z0, z1, x0, x1 = prepare(features, inv_gram)
    z_slots, z_mark = all_slots((z0, z1))
    x0, x1, _ = lax.optimization_barrier((x0, x1, z_mark))
    z_quarters = with_other_core(z_slots)

    def slot(b):
        return lax.rem(feat + (blocks - b), blocks)[None]

    def z_of(b, quarters):
        return gather(gather_z_kernel, [(block_width, both)] * 2, slot(b), quarters)

    def x_of(b, quarters):
        return gather(gather_x_kernel, [(both, block_width)], slot(b), quarters)[0]

    z_now = z_of(0, z_quarters)
    pieces = pl.pallas_call(
        functools.partial(first_kernel, slices),
        in_specs=[SMEM] + [VMEM] * 4,
        out_specs=VMEM,
        out_shape=held((chips, chunk + slices, LANES)),
        compiler_params=room(12),
    )(slice_index, lab_column, lab_row, *map(near, z_now))

    kept_rows = []
    kept_solved = []
    totals = weight = x_quarters = None
    for b in range(blocks):
        arrived = lax.all_to_all(pieces, XZ, 0, 0, tiled=True)
        if b == 0:
            tied = []

            def after_round(*parts):
                held_back = lax.optimization_barrier((*parts, arrived))
                tied.append(held_back[-1])
                return held_back[:-1]

            x_slots, _ = all_slots((x0, x1), after_round)
            arrived = tied[0]
            x_quarters = with_other_core(x_slots)
        result = middle(slices, total_rows, slice_index, arrived, chunk)
        kept_solved.append(result[0])
        if b == 0:
            totals = result[2]
        everyone = lax.all_to_all(result[1], XZ, 0, 0, tiled=True)
        x_now = x_of(b, x_quarters)
        if b < blocks - 1:
            z_now = z_of(b + 1, z_quarters)
        if b == 0:
            residual, weight, pieces = pl.pallas_call(
                functools.partial(second_kernel, slices, total_rows),
                in_specs=[SMEM] + [VMEM] * 6,
                out_specs=[VMEM] * 3,
                out_shape=[held((both, LANES)), held((both, LANES)), held((chips, chunk, LANES))],
                compiler_params=room(12),
            )(slice_index, lab_column, *map(near, (totals, everyone, x_now, *z_now)))
            kept_rows.append(residual)
        elif b < blocks - 1:
            residual, pieces = pl.pallas_call(
                step_kernel,
                in_specs=[VMEM] * 6,
                out_specs=[VMEM] * 2,
                out_shape=[held((both, LANES)), held((chips, chunk, LANES))],
                compiler_params=room(12),
            )(*map(near, (everyone, x_now, *z_now, kept_rows[-1], weight)))
            kept_rows.append(residual)
        else:
            sends = pl.pallas_call(
                functools.partial(last_kernel, blocks),
                in_specs=[SMEM] + [VMEM] * (2 + blocks + len(kept_rows)),
                out_specs=VMEM,
                out_shape=held((slices, chunk // cores + rows_here, LANES)),
                compiler_params=room(12),
            )(core_index, *map(near, (everyone, x_now, *kept_solved, *kept_rows)))

    got = near(lax.all_to_all(sends, ("feat", "core"), 0, 0, tiled=True))
    return pl.pallas_call(
        join_kernel,
        in_specs=[VMEM],
        out_specs=[VMEM, VMEM],
        out_shape=[
            jax.ShapeDtypeStruct((chunk // cores, C), F32),
            jax.ShapeDtypeStruct((1, rows_here, C), F32),
        ],
        compiler_params=room(12),
    )(got)


def solution(mesh):
    sizes = dict(mesh.shape)
    fine = Mesh(mesh.devices.reshape(sizes["feat"], 4, 8, 2), ("feat", "x", "z", "core"))
    rows = ("x", "z", "core")
    in_specs = (P(rows, "feat"), P(rows), P("feat", None, None))
    out_specs = (P(("feat",) + rows, None), P("feat", rows, None))
    return jax.shard_map(local, mesh=fine, in_specs=in_specs, out_specs=out_specs, check_vma=False)
```

```python
import functools

import jax
import jax.numpy as jnp
from jax import lax
from jax.experimental import pallas as pl
from jax.experimental.pallas import tpu as pltpu
from jax.sharding import Mesh, PartitionSpec as P


C = 640
LANES = 128
XZ = ("x", "z")
F32 = jnp.float32
BF16 = jnp.bfloat16
VMEM = pl.BlockSpec(memory_space=pltpu.VMEM)
SMEM = pl.BlockSpec(memory_space=pltpu.SMEM)


def room(mib):
    return pltpu.CompilerParams(vmem_limit_bytes=mib << 20)


def dot(left, right):
    return jnp.dot(left, right, preferred_element_type=F32)


def dot_t(left, right):
    return lax.dot_general(left, right, (((1,), (1,)), ((), ())), preferred_element_type=F32)


def swap_cores(value):
    return lax.ppermute(value, "core", [(0, 1), (1, 0)])


def prepare_kernel(gram_ref, x_ref, z0_ref, z1_ref, x0_ref, x1_ref):
    step = pl.program_id(0)
    gram = gram_ref[0]
    high = gram.astype(BF16)
    rest = gram - high.astype(F32)
    mid = rest.astype(BF16)
    low = (rest - mid.astype(F32)).astype(BF16)
    x = x_ref[...]
    zt = (dot_t(low, x) + dot_t(mid, x)) + dot_t(high, x)
    tile = zt.shape[0]
    per_half = z0_ref.shape[0] // tile

    @pl.when(step < per_half)
    def _():
        z0_ref[pl.ds(pl.multiple_of(step * tile, tile), tile), :] = zt

    @pl.when(step >= per_half)
    def _():
        z1_ref[pl.ds(pl.multiple_of((step - per_half) * tile, tile), tile), :] = zt

    @pl.when(step == 0)
    def _():
        half = x0_ref.shape[0]
        x0_ref[...] = x[:half].astype(F32)
        x1_ref[...] = x[half:].astype(F32)


def prepare(features, inv_gram, tile=256):
    rows, width = features.shape
    z_shape = (width // 2, rows)
    x_shape = (rows // 2, width)
    return pl.pallas_call(
        prepare_kernel,
        grid=(width // tile,),
        in_specs=[
            pl.BlockSpec((1, tile, width), lambda i: (0, i, 0)),
            pl.BlockSpec((rows, width), lambda i: (0, 0)),
        ],
        out_specs=[pl.BlockSpec(z_shape, lambda i: (0, 0))] * 2
        + [pl.BlockSpec(x_shape, lambda i: (0, 0))] * 2,
        out_shape=[jax.ShapeDtypeStruct(z_shape, F32)] * 2
        + [jax.ShapeDtypeStruct(x_shape, F32)] * 2,
        compiler_params=room(24),
    )(inv_gram, features)


def held(shape, dtype=F32):
    return pltpu.VMEM(shape, dtype)


def near(value):
    return pltpu.with_memory_space_constraint(value, pltpu.VMEM)


def far(value):
    return pltpu.with_memory_space_constraint(value, pltpu.HBM)


ANY = pl.BlockSpec(memory_space=pl.ANY)


def start_fetch(slot_ref, refs, landing, sems):
    for slot in range(len(refs) // 4):

        @pl.when(slot_ref[0] == slot)
        def _():
            for q in range(4):
                pltpu.make_async_copy(refs[slot * 4 + q], landing.at[q], sems.at[q]).start()


def wait_fetch(refs, landing, sems):
    for q in range(4):
        pltpu.make_async_copy(refs[q], landing.at[q], sems.at[q]).wait()


def landing_of(quarters):
    return [pltpu.VMEM((4,) + quarters[0].shape, F32), pltpu.SemaphoreType.DMA((4,))]


def partial_sum(landing, scaled):
    half = scaled.shape[0] // 2
    parts = []
    for h in range(2):
        total = None
        for k in range(2):
            value = landing[k * 2 + h]
            high = value.astype(BF16)
            low = (value - high.astype(F32)).astype(BF16)
            right = scaled[k * half : (k + 1) * half]
            part = dot(low, right) + dot(high, right)
            total = part if total is None else total + part
        parts.append(total)
    return parts


def put_pieces(out_ref, parts, chunk):
    for h, part in enumerate(parts):
        count = part.shape[0] // chunk
        out_ref[h * count : (h + 1) * count, :chunk, :] = part.reshape(count, chunk, LANES)


def label_parts(lab, slices, width):
    group = jnp.zeros_like(lab)
    for d in range(1, slices):
        group = group + (lab >= d * width).astype(jnp.int32)
    return group, lab - group * width


def first_kernel(slices, slice_ref, slot_ref, lab_ref, labt_ref, *refs):
    z_refs, (out_ref, landing, sems) = refs[:-3], refs[-3:]
    start_fetch(slot_ref, z_refs, landing, sems)
    width = C // slices
    lab = lab_ref[...]
    group, low_label = label_parts(lab, slices, width)
    lane = lax.broadcasted_iota(jnp.int32, (lab.shape[0], LANES), 1)
    low_hot = jnp.where(low_label == lane, 1.0, 0.0)
    onehot = jnp.where(group == slice_ref[0], low_hot, 0.0).astype(BF16)
    labt = labt_ref[...]
    first = lax.broadcasted_iota(jnp.int32, (slices, labt.shape[1]), 0) * width
    group_hot = jnp.where((labt >= first) & (labt < first + width), 1.0, 0.0).astype(BF16)
    counts = dot(group_hot, low_hot.astype(BF16))
    chips, deep, _ = out_ref.shape
    out_ref[:, deep - slices :, :] = jnp.broadcast_to(counts[None], (chips, slices, LANES))
    wait_fetch(z_refs, landing, sems)
    put_pieces(out_ref, partial_sum(landing, onehot), deep - slices)


def middle_kernel(total_rows, slice_ref, in_ref, *out_refs):
    summed = jnp.sum(in_ref[...], axis=0)
    solved_ref, copies_ref = out_refs[0], out_refs[1]
    chunk = solved_ref.shape[0]
    solved = summed[:chunk]
    if len(out_refs) == 3:
        totals = summed[chunk:]
        out_refs[2][...] = totals
        row = lax.broadcasted_iota(jnp.int32, totals.shape, 0)
        mine = jnp.sum(jnp.where(row == slice_ref[0], totals, 0.0), axis=0, keepdims=True)
        scale = jnp.where(mine > 0.0, total_rows / (C * jnp.maximum(mine, 1.0)), 0.0)
        solved = solved * scale.astype(BF16).astype(F32)
    solved_ref[...] = solved
    copies_ref[...] = jnp.broadcast_to(solved[None], copies_ref.shape)


def middle(slices, total_rows, slice_index, arrived, chunk):
    chips, deep, _ = arrived.shape
    shapes = [held((chunk, LANES)), held((chips, chunk, LANES))]
    if deep > chunk:
        shapes.append(held((slices, LANES)))
    return pl.pallas_call(
        functools.partial(middle_kernel, total_rows),
        in_specs=[SMEM, VMEM],
        out_specs=[VMEM] * len(shapes),
        out_shape=shapes,
        compiler_params=room(8),
    )(slice_index, near(arrived))


def update(everyone_ref, landing, residual):
    solved = everyone_ref[...].reshape(-1, LANES).astype(BF16)
    product = dot(landing[...].reshape(-1, landing.shape[2]).astype(BF16), solved)
    return residual - product


def second_kernel(
    slices, total_rows, count, slice_ref, x_slot_ref, z_slot_ref, lab_ref, totals_ref,
    everyone_ref, *refs,
):
    x_refs, z_refs = refs[:count], refs[count : 2 * count]
    residual_ref, weight_ref, out_ref, x_land, x_sems, z_land, z_sems = refs[2 * count :]
    start_fetch(x_slot_ref, x_refs, x_land, x_sems)
    start_fetch(z_slot_ref, z_refs, z_land, z_sems)
    width = C // slices
    lab = lab_ref[...]
    group, low_label = label_parts(lab, slices, width)
    lane = lax.broadcasted_iota(jnp.int32, (lab.shape[0], LANES), 1)
    hit = low_label == lane
    spread = jnp.zeros((lab.shape[0], LANES), F32)
    for d in range(slices):
        spread = jnp.where(group == d, totals_ref[d : d + 1, :], spread)
    row_count = jnp.sum(jnp.where(hit, spread, 0.0), axis=1, keepdims=True)
    weight = total_rows / (C * row_count)
    weight_ref[...] = jnp.broadcast_to(weight, weight_ref.shape)
    onehot = jnp.where(hit & (group == slice_ref[0]), 1.0, 0.0)
    wait_fetch(x_refs, x_land, x_sems)
    residual = update(everyone_ref, x_land, onehot)
    residual_ref[...] = residual
    wait_fetch(z_refs, z_land, z_sems)
    put_pieces(out_ref, partial_sum(z_land, (weight * residual).astype(BF16)), out_ref.shape[1])


def step_kernel(count, x_slot_ref, z_slot_ref, everyone_ref, old_ref, weight_ref, *refs):
    x_refs, z_refs = refs[:count], refs[count : 2 * count]
    residual_ref, out_ref, x_land, x_sems, z_land, z_sems = refs[2 * count :]
    start_fetch(x_slot_ref, x_refs, x_land, x_sems)
    start_fetch(z_slot_ref, z_refs, z_land, z_sems)
    wait_fetch(x_refs, x_land, x_sems)
    residual = update(everyone_ref, x_land, old_ref[...])
    residual_ref[...] = residual
    scaled = (weight_ref[...] * residual).astype(BF16)
    wait_fetch(z_refs, z_land, z_sems)
    put_pieces(out_ref, partial_sum(z_land, scaled), out_ref.shape[1])


def last_kernel(blocks, count, core_ref, x_slot_ref, everyone_ref, *refs):
    solved_refs, refs = refs[:blocks], refs[blocks:]
    rows_refs, refs = refs[: blocks - 1], refs[blocks - 1 :]
    x_refs, (out_ref, x_land, x_sems) = refs[:count], refs[count:]
    start_fetch(x_slot_ref, x_refs, x_land, x_sems)
    rows = rows_refs[0].shape[0] // 2
    half = solved_refs[0].shape[0] // 2
    for b in range(blocks):
        for k in range(2):
            out_ref[2 * b + k, :half] = solved_refs[b][k * half : (k + 1) * half]
            if b < blocks - 1:
                begin = pl.multiple_of(jnp.where(core_ref[0] == k, 0, rows), rows)
                out_ref[2 * b + k, half:] = rows_refs[b][pl.ds(begin, rows), :]
    wait_fetch(x_refs, x_land, x_sems)
    last = update(everyone_ref, x_land, rows_refs[-1][...])
    for k in range(2):
        mine = jnp.where(core_ref[0] == k, last[:rows], last[rows:])
        out_ref[2 * blocks - 2 + k, half:] = mine


def join_kernel(in_ref, weights_ref, after_ref):
    slices = in_ref.shape[0]
    width = C // slices
    head = weights_ref.shape[0]
    for d in range(slices):
        weights_ref[:, d * width : (d + 1) * width] = in_ref[d, :head, :width]
        after_ref[0, :, d * width : (d + 1) * width] = in_ref[d, head:, :width]


def shifted(value, by):
    count = lax.axis_size("feat")
    return lax.ppermute(value, "feat", [(i, (i + by) % count) for i in range(count)])


def exchange(value):
    return lax.all_to_all(value, XZ, 0, 0, tiled=True)


def tie(values, *others):
    return lax.optimization_barrier((*values, *others))[: len(values)]


def local(features, labels, inv_gram):
    rows_here, block_width = features.shape
    blocks = lax.axis_size("feat")
    cores = lax.axis_size("core")
    chips = lax.axis_size("x") * lax.axis_size("z")
    slices = blocks * cores
    chunk = block_width // chips
    core = lax.axis_index("core").astype(jnp.int32)
    feat = lax.axis_index("feat").astype(jnp.int32)
    core_index = core[None]
    slice_index = (feat * cores + core)[None]
    total_rows = float(rows_here * chips * cores)
    both = cores * rows_here

    def slot(b):
        return lax.rem(feat + (blocks - b), blocks)[None]

    z0, z1, x0, x1 = prepare(features, inv_gram)
    lab_other = swap_cores(labels)
    lab = jnp.concatenate([labels, lab_other])
    lab_column, lab_row = lab[:, None], lab[None, :]

    z_up0, z_down1 = shifted(z0, 1), shifted(z1, -1)
    z0s, z1s = swap_cores(z0), swap_cores(z1)
    z0_late, z1_late = tie((z0, z1), z0s, z1s)
    z_up1, z_down0 = shifted(z1_late, 1), shifted(z0_late, -1)
    z_far0, z_far1 = shifted(z_up0, 1), shifted(z_down1, -1)
    x0, x1 = tie((x0, x1), z_up0, z_down1)
    z_all = [
        z0, z1, z0s, z1s,
        z_up0, z_up1, swap_cores(z_up0), swap_cores(z_up1),
        z_far0, z_far1, swap_cores(z_far0), swap_cores(z_far1),
        z_down0, z_down1, swap_cores(z_down0), swap_cores(z_down1),
    ]
    z_all = [far(z) for z in z_all]
    x0s, x1s = swap_cores(x0), swap_cores(x1)
    x_up0, x_down1 = shifted(x0, 1), shifted(x1, -1)
    x0_late, x1_late = tie((x0, x1), x0s, x1s)
    x_up1 = shifted(x1_late, 1)
    x_down0 = shifted(x0_late, -1)

    pieces = pl.pallas_call(
        functools.partial(first_kernel, slices),
        in_specs=[SMEM, SMEM, VMEM, VMEM] + [ANY] * len(z_all),
        out_specs=VMEM,
        out_shape=held((chips, chunk + slices, LANES)),
        scratch_shapes=landing_of(z_all),
        compiler_params=room(12),
    )(slice_index, slot(0), lab_column, lab_row, *z_all)

    kept_rows = []
    kept_solved = []
    totals = weight = x_all = None
    for b in range(blocks):
        arrived = exchange(pieces)
        if b == 0:
            arrived, x_up0, x_down1, x_up1, x_down0 = lax.optimization_barrier(
                (arrived, x_up0, x_down1, x_up1, x_down0)
            )
            x_far0, x_far1 = shifted(x_up0, 1), shifted(x_down1, -1)
            x_near = [x_up0, x_up1, swap_cores(x_up0), swap_cores(x_up1)]
            x_next = [x_down0, x_down1, swap_cores(x_down0), swap_cores(x_down1)]
        result = middle(slices, total_rows, slice_index, arrived, chunk)
        kept_solved.append(result[0])
        if b == 0:
            totals = result[2]
        everyone = exchange(result[1])
        if b == 0:
            everyone, x_far0, x_far1, *x_others = lax.optimization_barrier(
                (everyone, x_far0, x_far1, *x_near, *x_next)
            )
            x_all = [x0, x1, x0s, x1s, *x_others[:4]]
            x_all += [x_far0, x_far1, swap_cores(x_far0), swap_cores(x_far1), *x_others[4:]]
            x_all = [far(x) for x in x_all]
        count = len(x_all)
        if b == 0:
            residual, weight, pieces = pl.pallas_call(
                functools.partial(second_kernel, slices, total_rows, count),
                in_specs=[SMEM] * 3 + [VMEM] * 3 + [ANY] * 2 * count,
                out_specs=[VMEM] * 3,
                out_shape=[held((both, LANES)), held((both, LANES)), held((chips, chunk, LANES))],
                scratch_shapes=landing_of(x_all) + landing_of(z_all),
                compiler_params=room(16),
            )(slice_index, slot(b), slot(b + 1), lab_column, near(totals), near(everyone),
              *x_all, *z_all)
            kept_rows.append(residual)
        elif b < blocks - 1:
            residual, pieces = pl.pallas_call(
                functools.partial(step_kernel, count),
                in_specs=[SMEM] * 2 + [VMEM] * 3 + [ANY] * 2 * count,
                out_specs=[VMEM] * 2,
                out_shape=[held((both, LANES)), held((chips, chunk, LANES))],
                scratch_shapes=landing_of(x_all) + landing_of(z_all),
                compiler_params=room(16),
            )(slot(b), slot(b + 1), near(everyone), near(kept_rows[-1]), near(weight),
              *x_all, *z_all)
            kept_rows.append(residual)
        else:
            sends = pl.pallas_call(
                functools.partial(last_kernel, blocks, count),
                in_specs=[SMEM] * 2 + [VMEM] * (1 + blocks + len(kept_rows)) + [ANY] * count,
                out_specs=VMEM,
                out_shape=held((slices, chunk // cores + rows_here, LANES)),
                scratch_shapes=landing_of(x_all),
                compiler_params=room(12),
            )(core_index, slot(b), *map(near, (everyone, *kept_solved, *kept_rows)), *x_all)

    got = near(lax.all_to_all(sends, ("feat", "core"), 0, 0, tiled=True))
    return pl.pallas_call(
        join_kernel,
        in_specs=[VMEM],
        out_specs=[VMEM, VMEM],
        out_shape=[
            jax.ShapeDtypeStruct((chunk // cores, C), F32),
            jax.ShapeDtypeStruct((1, rows_here, C), F32),
        ],
        compiler_params=room(12),
    )(got)


def solution(mesh):
    sizes = dict(mesh.shape)
    fine = Mesh(mesh.devices.reshape(sizes["feat"], 4, 8, 2), ("feat", "x", "z", "core"))
    rows = ("x", "z", "core")
    in_specs = (P(rows, "feat"), P(rows), P("feat", None, None))
    out_specs = (P(("feat",) + rows, None), P("feat", rows, None))

    return jax.shard_map(local, mesh=fine, in_specs=in_specs, out_specs=out_specs, check_vma=False)
```

```python
import functools

import jax
import jax.numpy as jnp
from jax import lax
from jax.experimental import pallas as pl
from jax.experimental.pallas import tpu as pltpu
from jax.sharding import Mesh, PartitionSpec as P


C = 640
LANES = 128
ROW_TILE = 8
XZ = ("x", "z")
F32 = jnp.float32
BF16 = jnp.bfloat16
VMEM = pl.BlockSpec(memory_space=pltpu.VMEM)
SMEM = pl.BlockSpec(memory_space=pltpu.SMEM)
ANY = pl.BlockSpec(memory_space=pl.ANY)


def room(mib):
    return pltpu.CompilerParams(vmem_limit_bytes=mib << 20)


def dot_t(left, right):
    return lax.dot_general(left, right, (((1,), (1,)), ((), ())), preferred_element_type=F32)


def swap_cores(value):
    return lax.ppermute(value, "core", [(0, 1), (1, 0)])


def prepare_kernel(gram_ref, x_ref, z_ref, xf_ref):
    gram = gram_ref[0]
    high = gram.astype(BF16)
    rest = gram - high.astype(F32)
    mid = rest.astype(BF16)
    low = (rest - mid.astype(F32)).astype(BF16)
    x = x_ref[...]
    z_ref[...] = (dot_t(low, x) + dot_t(mid, x)) + dot_t(high, x)

    @pl.when(pl.program_id(0) == 0)
    def _():
        xf_ref[...] = x.astype(F32)


def prepare(features, inv_gram, tile=256):
    rows, width = features.shape
    return pl.pallas_call(
        prepare_kernel,
        grid=(width // tile,),
        in_specs=[
            pl.BlockSpec((1, tile, width), lambda i: (0, i, 0)),
            pl.BlockSpec((rows, width), lambda i: (0, 0)),
        ],
        out_specs=[
            pl.BlockSpec((tile, rows), lambda i: (i, 0)),
            pl.BlockSpec((rows, width), lambda i: (0, 0)),
        ],
        out_shape=[
            jax.ShapeDtypeStruct((width, rows), F32),
            jax.ShapeDtypeStruct((rows, width), F32),
        ],
        compiler_params=room(24),
    )(inv_gram, features)


def held(shape, dtype=F32):
    return pltpu.VMEM(shape, dtype)


def near(value):
    return pltpu.with_memory_space_constraint(value, pltpu.VMEM)


def far(value):
    return pltpu.with_memory_space_constraint(value, pltpu.HBM)


HELD_BLOCKS = 10


def fetch(slot_ref, refs, landing, sems):
    half = landing.shape[1] // 2
    for slot, first in ((0, 0), (1, 2), (3, 4)):

        @pl.when(slot_ref[0] == slot)
        def _():
            for k in range(2):
                pltpu.make_async_copy(refs[first + k], landing.at[k], sems.at[k]).start()

    @pl.when(slot_ref[0] == 2)
    def _():
        for k in range(2):
            for h in range(2):
                target = landing.at[k, pl.ds(h * half, half)]
                pltpu.make_async_copy(refs[6 + 2 * k + h], target, sems.at[k]).start()


def wait_fetch(refs, landing, sems):
    for k in range(2):
        pltpu.make_async_copy(refs[k], landing.at[k], sems.at[k]).wait()


def landing_of(blocks):
    return [pltpu.VMEM((2,) + blocks[0].shape, F32), pltpu.SemaphoreType.DMA((2,))]


def partial_sum(landing, scaled):
    half = scaled.shape[1] // 2
    total = None
    for k in range(2):
        value = landing[k]
        high = value.astype(BF16)
        low = (value - high.astype(F32)).astype(BF16)
        left = scaled[:, k * half : (k + 1) * half]
        part = dot_t(left, low) + dot_t(left, high)
        total = part if total is None else total + part
    return total


def put_pieces(out_ref, total, chunk):
    tiles = total.shape[1] // LANES
    for g in range(total.shape[0] // chunk):
        for t in range(tiles):
            out_ref[g * tiles + t, :chunk, :] = total[
                g * chunk : (g + 1) * chunk, t * LANES : (t + 1) * LANES
            ]


def take_copies(everyone_ref, groups):
    tiles = everyone_ref.shape[0] // groups
    rows = []
    for g in range(groups):
        rows.append(
            jnp.concatenate([everyone_ref[g * tiles + t] for t in range(tiles)], axis=1)
        )
    return jnp.concatenate(rows, axis=0)


def label_parts(lab, slices, width):
    group = jnp.zeros_like(lab)
    for d in range(1, slices):
        group = group + (lab >= d * width).astype(jnp.int32)
    return group, lab - group * width


def first_kernel(slices, padded, slice_ref, slot_ref, lab_ref, *refs):
    z_refs, (out_ref, landing, sems) = refs[:-3], refs[-3:]
    fetch(slot_ref, z_refs, landing, sems)
    lab = lab_ref[...]
    group, low_label = label_parts(lab, slices, C // slices)
    row = lax.broadcasted_iota(jnp.int32, (LANES, lab.shape[1]), 0)
    low_hot = jnp.where(low_label == row, 1.0, 0.0)
    onehot = jnp.where(group == slice_ref[0], low_hot, 0.0)[:padded].astype(BF16)
    group_row = lax.broadcasted_iota(jnp.int32, (slices, lab.shape[1]), 0)
    group_hot = jnp.where(group == group_row, 1.0, 0.0).astype(BF16)
    counts = dot_t(group_hot, low_hot.astype(BF16))
    chips, deep, _ = out_ref.shape
    chunk = deep - slices
    out_ref[:, chunk:, :] = jnp.broadcast_to(counts[None], (chips, slices, LANES))
    wait_fetch(z_refs, landing, sems)
    put_pieces(out_ref, partial_sum(landing, onehot), chunk)


def middle_kernel(total_rows, slice_ref, part_ref, in_ref, *out_refs):
    summed = jnp.sum(in_ref[...], axis=0)
    copies_ref = out_refs[0]
    chunk = copies_ref.shape[1]
    solved = summed[:chunk]
    if len(out_refs) == 2:
        totals = summed[chunk:]
        out_refs[1][...] = totals
        row = lax.broadcasted_iota(jnp.int32, totals.shape, 0)
        mine = jnp.sum(jnp.where(row == slice_ref[0], totals, 0.0), axis=0, keepdims=True)
        scale = jnp.where(mine > 0.0, total_rows / (C * jnp.maximum(mine, 1.0)), 0.0)
        scale = scale.astype(BF16).astype(F32)
        lane = lax.broadcasted_iota(jnp.int32, (chunk, LANES), 1)
        here = lax.broadcasted_iota(jnp.int32, (chunk, LANES), 0) + part_ref[0] * chunk
        solved = solved * jnp.sum(jnp.where(lane == here, scale, 0.0), axis=1, keepdims=True)
    copies_ref[...] = jnp.broadcast_to(solved[None], copies_ref.shape)


def middle(slices, total_rows, slice_index, part_index, arrived, chunk):
    chips, deep, _ = arrived.shape
    shapes = [held((chips, chunk, LANES))]
    if deep > chunk:
        shapes.append(held((slices, LANES)))
    return pl.pallas_call(
        functools.partial(middle_kernel, total_rows),
        in_specs=[SMEM, SMEM, VMEM],
        out_specs=[VMEM] * len(shapes),
        out_shape=shapes,
        compiler_params=room(8),
    )(slice_index, part_index, near(arrived))


def update(solved, landing, residual):
    rows = landing.shape[1]
    solved = solved.astype(BF16)
    parts = [
        residual[:, k * rows : (k + 1) * rows] - dot_t(solved, landing[k].astype(BF16))
        for k in range(2)
    ]
    return jnp.concatenate(parts, axis=1)


def second_kernel(
    slices, total_rows, groups, slice_ref, x_slot_ref, z_slot_ref, lab_ref, totals_ref,
    everyone_ref, *refs,
):
    x_refs, z_refs = refs[:HELD_BLOCKS], refs[HELD_BLOCKS : 2 * HELD_BLOCKS]
    solved_ref, residual_ref, weight_ref, out_ref = refs[2 * HELD_BLOCKS : 2 * HELD_BLOCKS + 4]
    x_land, x_sems, z_land, z_sems = refs[2 * HELD_BLOCKS + 4 :]
    fetch(x_slot_ref, x_refs, x_land, x_sems)
    fetch(z_slot_ref, z_refs, z_land, z_sems)
    lab = lab_ref[...]
    group, low_label = label_parts(lab, slices, C // slices)
    solved = take_copies(everyone_ref, groups)
    solved_ref[...] = solved
    padded = solved.shape[0]
    row = lax.broadcasted_iota(jnp.int32, (padded, lab.shape[1]), 0)
    hit = low_label == row
    columns = totals_ref[...].T
    spread = jnp.zeros((padded, lab.shape[1]), F32)
    for d in range(slices):
        spread = jnp.where(group == d, columns[:padded, d : d + 1], spread)
    row_count = jnp.sum(jnp.where(hit, spread, 0.0), axis=0, keepdims=True)
    weight = total_rows / (C * row_count)
    weight_ref[...] = jnp.broadcast_to(weight, weight_ref.shape)
    onehot = jnp.where(hit & (group == slice_ref[0]), 1.0, 0.0)
    wait_fetch(x_refs, x_land, x_sems)
    residual = update(solved, x_land, onehot)
    residual_ref[...] = residual
    wait_fetch(z_refs, z_land, z_sems)
    put_pieces(out_ref, partial_sum(z_land, (weight * residual).astype(BF16)), out_ref.shape[1])


def step_kernel(groups, x_slot_ref, z_slot_ref, everyone_ref, old_ref, weight_ref, *refs):
    x_refs, z_refs = refs[:HELD_BLOCKS], refs[HELD_BLOCKS : 2 * HELD_BLOCKS]
    solved_ref, residual_ref, out_ref = refs[2 * HELD_BLOCKS : 2 * HELD_BLOCKS + 3]
    x_land, x_sems, z_land, z_sems = refs[2 * HELD_BLOCKS + 3 :]
    fetch(x_slot_ref, x_refs, x_land, x_sems)
    fetch(z_slot_ref, z_refs, z_land, z_sems)
    solved = take_copies(everyone_ref, groups)
    solved_ref[...] = solved
    wait_fetch(x_refs, x_land, x_sems)
    residual = update(solved, x_land, old_ref[...])
    residual_ref[...] = residual
    scaled = (weight_ref[0:1, :] * residual).astype(BF16)
    wait_fetch(z_refs, z_land, z_sems)
    put_pieces(out_ref, partial_sum(z_land, scaled), out_ref.shape[1])


def last_kernel(
    blocks, groups, width, place_ref, x_slot_ref, everyone_ref, *refs,
):
    solved_refs, refs = refs[: blocks - 1], refs[blocks - 1 :]
    rows_refs, refs = refs[: blocks - 1], refs[blocks - 1 :]
    x_refs, (out_ref, x_land, x_sems, turned) = refs[:HELD_BLOCKS], refs[HELD_BLOCKS:]
    fetch(x_slot_ref, x_refs, x_land, x_sems)
    last_solved = take_copies(everyone_ref, groups)
    rows = x_land.shape[1]
    head = out_ref.shape[1] - width
    share = 2 * head
    for b in range(blocks):
        solved = last_solved if b == blocks - 1 else solved_refs[b][...]
        tile = jnp.zeros((solved.shape[0], LANES), F32)
        for t in range(solved.shape[1] // LANES):
            tile = jnp.where(place_ref[1] == t, solved[:, t * LANES : (t + 1) * LANES], tile)
        empty = jnp.zeros((LANES - tile.shape[0], LANES), F32)
        turned[...] = jnp.concatenate([tile, empty], axis=0).T
        for k in range(2):
            begin = place_ref[2] * (2 * share) + k * share
            begin = pl.multiple_of(begin, ROW_TILE)
            for h in range(2):
                out_ref[2 * b + k, :head, h * LANES : (h + 1) * LANES] = turned[
                    pl.ds(pl.multiple_of(begin + h * head, ROW_TILE), head), :
                ]
    wait_fetch(x_refs, x_land, x_sems)
    last = update(last_solved, x_land, rows_refs[-1][...])
    for b in range(blocks):
        value = last if b == blocks - 1 else rows_refs[b][...]
        for k in range(2):
            mine = jnp.where(place_ref[0] == k, value[:width, :rows], value[:width, rows:])
            out_ref[2 * b + k, head:, :] = mine


def join_kernel(in_ref, weights_ref, after_ref):
    slices, deep, _ = in_ref.shape
    width = C // slices
    head = deep - width
    for d in range(slices):
        for h in range(2):
            weights_ref[h * head : (h + 1) * head, d * width : (d + 1) * width] = in_ref[
                d, :head, h * LANES : h * LANES + width
            ]
    joined = jnp.concatenate([in_ref[d, head:, :] for d in range(slices)], axis=0)
    after_ref[0] = joined.T


def shifted(value, by):
    count = lax.axis_size("feat")
    return lax.ppermute(value, "feat", [(i, (i + by) % count) for i in range(count)])


def exchange(value):
    return lax.all_to_all(value, XZ, 0, 0, tiled=True)


def halves(value):
    middle_row = value.shape[0] // 2
    return value[:middle_row], value[middle_row:]


def local(features, labels, inv_gram):
    rows_here, block_width = features.shape
    blocks = lax.axis_size("feat")
    cores = lax.axis_size("core")
    groups = lax.axis_size("x")
    depth = lax.axis_size("z")
    chips = groups * depth
    slices = blocks * cores
    width = C // slices
    tile_rows = groups * ROW_TILE
    padded = -(-width // tile_rows) * tile_rows
    chunk = padded // groups
    core = lax.axis_index("core").astype(jnp.int32)
    feat = lax.axis_index("feat").astype(jnp.int32)
    x_index = lax.axis_index("x").astype(jnp.int32)
    chip = x_index * depth + lax.axis_index("z").astype(jnp.int32)
    per_tile = LANES * chips // block_width
    place = jnp.stack([core, chip // per_tile, chip % per_tile])
    slice_index = (feat * cores + core)[None]
    part_index = x_index[None]
    total_rows = float(rows_here * chips * cores)
    both = cores * rows_here

    def slot(b):
        return lax.rem(feat + (blocks - b), blocks)[None]

    z_own, x_own = prepare(features, inv_gram)
    lab = jnp.concatenate([labels, swap_cores(labels)])[None, :]

    z_up, z_down = shifted(z_own, 1), shifted(z_own, -1)
    z_pair = [z_own, swap_cores(z_own)]
    z_far0 = shifted(halves(z_up)[0], 1)
    z_far1 = shifted(halves(z_down)[1], -1)
    x_own, _, _ = lax.optimization_barrier((x_own, z_up, z_down))
    z_all = z_pair + [z_up, swap_cores(z_up), z_down, swap_cores(z_down)]
    z_all += [z_far0, z_far1, swap_cores(z_far0), swap_cores(z_far1)]
    z_all = [far(z) for z in z_all]
    x_up, x_down = shifted(x_own, 1), shifted(x_own, -1)

    pieces = pl.pallas_call(
        functools.partial(first_kernel, slices, padded),
        in_specs=[SMEM, SMEM, VMEM] + [ANY] * HELD_BLOCKS,
        out_specs=VMEM,
        out_shape=held((chips, chunk + slices, LANES)),
        scratch_shapes=landing_of(z_all),
        compiler_params=room(12),
    )(slice_index, slot(0), lab, *z_all)

    rows_shape = held((padded, both))
    solved_shape = held((padded, block_width))
    pieces_shape = held((chips, chunk, LANES))
    kept_rows = []
    kept_solved = []
    totals = weight = x_all = x_near = None
    for b in range(blocks):
        arrived = exchange(pieces)
        if b == 0:
            arrived, x_up, x_down, x_own = lax.optimization_barrier(
                (arrived, x_up, x_down, x_own)
            )
            x_far0 = shifted(halves(x_up)[0], 1)
            x_far1 = shifted(halves(x_down)[1], -1)
            x_near = [x_own, swap_cores(x_own), x_up, swap_cores(x_up)]
            x_near += [x_down, swap_cores(x_down)]
        result = middle(slices, total_rows, slice_index, part_index, arrived, chunk)
        if b == 0:
            totals = result[1]
        everyone = exchange(result[0])
        if b == 0:
            everyone, x_far0, x_far1, *x_near = lax.optimization_barrier(
                (everyone, x_far0, x_far1, *x_near)
            )
            x_all = x_near + [x_far0, x_far1, swap_cores(x_far0), swap_cores(x_far1)]
            x_all = [far(x) for x in x_all]
            solved, residual, weight, pieces = pl.pallas_call(
                functools.partial(second_kernel, slices, total_rows, groups),
                in_specs=[SMEM] * 3 + [VMEM] * 3 + [ANY] * 2 * HELD_BLOCKS,
                out_specs=[VMEM] * 4,
                out_shape=[solved_shape, rows_shape, held((ROW_TILE, both)), pieces_shape],
                scratch_shapes=landing_of(x_all) + landing_of(z_all),
                compiler_params=room(16),
            )(slice_index, slot(b), slot(b + 1), lab, near(totals), near(everyone),
              *x_all, *z_all)
        elif b < blocks - 1:
            solved, residual, pieces = pl.pallas_call(
                functools.partial(step_kernel, groups),
                in_specs=[SMEM] * 2 + [VMEM] * 3 + [ANY] * 2 * HELD_BLOCKS,
                out_specs=[VMEM] * 3,
                out_shape=[solved_shape, rows_shape, pieces_shape],
                scratch_shapes=landing_of(x_all) + landing_of(z_all),
                compiler_params=room(16),
            )(slot(b), slot(b + 1), near(everyone), near(kept_rows[-1]), near(weight),
              *x_all, *z_all)
        else:
            head = block_width // (chips * cores) // 2
            sends = pl.pallas_call(
                functools.partial(last_kernel, blocks, groups, width),
                in_specs=[SMEM] * 2 + [VMEM] * (2 * blocks - 1) + [ANY] * HELD_BLOCKS,
                out_specs=VMEM,
                out_shape=held((slices, head + width, rows_here)),
                scratch_shapes=landing_of(x_all) + [pltpu.VMEM((LANES, LANES), F32)],
                compiler_params=room(14),
            )(place, slot(b), *map(near, (everyone, *kept_solved, *kept_rows)), *x_all)
        if b < blocks - 1:
            kept_solved.append(solved)
            kept_rows.append(residual)

    got = near(lax.all_to_all(sends, ("feat", "core"), 0, 0, tiled=True))
    return pl.pallas_call(
        join_kernel,
        in_specs=[VMEM],
        out_specs=[VMEM, VMEM],
        out_shape=[
            jax.ShapeDtypeStruct((block_width // (chips * cores), C), F32),
            jax.ShapeDtypeStruct((1, rows_here, C), F32),
        ],
        compiler_params=room(12),
    )(got)


def solution(mesh):
    sizes = dict(mesh.shape)
    fine = Mesh(mesh.devices.reshape(sizes["feat"], 4, 8, 2), ("feat", "x", "z", "core"))
    rows = ("x", "z", "core")
    in_specs = (P(rows, "feat"), P(rows), P("feat", None, None))
    out_specs = (P(("feat",) + rows, None), P("feat", rows, None))

    return jax.shard_map(local, mesh=fine, in_specs=in_specs, out_specs=out_specs, check_vma=False)
```

```python
import functools

import jax
import jax.numpy as jnp
from jax import lax
from jax.experimental import pallas as pl
from jax.experimental.pallas import tpu as pltpu
from jax.sharding import Mesh, PartitionSpec as P


C = 640
LANES = 128
ROW_TILE = 8
XZ = ("x", "z")
F32 = jnp.float32
BF16 = jnp.bfloat16
VMEM = pl.BlockSpec(memory_space=pltpu.VMEM)
SMEM = pl.BlockSpec(memory_space=pltpu.SMEM)
ANY = pl.BlockSpec(memory_space=pl.ANY)


def room(mib):
    return pltpu.CompilerParams(vmem_limit_bytes=mib << 20)


def dot_t(left, right):
    return lax.dot_general(left, right, (((1,), (1,)), ((), ())), preferred_element_type=F32)


def swap_cores(value):
    return lax.ppermute(value, "core", [(0, 1), (1, 0)])


def prepare_kernel(gram_ref, x_ref, z0_ref, z1_ref, xf_ref, gram_land, x_land, sems):
    tiles, tile, _ = gram_land.shape
    x_copy = pltpu.make_async_copy(x_ref, x_land, sems.at[tiles])
    x_copy.start()
    copies = []
    for t in range(tiles):
        source = gram_ref.at[0, pl.ds(t * tile, tile)]
        copies.append(pltpu.make_async_copy(source, gram_land.at[t], sems.at[t]))
        copies[t].start()
    x_copy.wait()
    x = x_land[...]
    per_half = tiles // 2
    for t in range(tiles):
        copies[t].wait()
        gram = gram_land[t]
        high = gram.astype(BF16)
        rest = gram - high.astype(F32)
        mid = rest.astype(BF16)
        low = (rest - mid.astype(F32)).astype(BF16)
        z_ref = z0_ref if t < per_half else z1_ref
        at = pl.ds((t % per_half) * tile, tile)
        z_ref[at, :] = (dot_t(low, x) + dot_t(mid, x)) + dot_t(high, x)
    xf_ref[...] = x.astype(F32)


def prepare(features, inv_gram, tiles=4):
    rows, width = features.shape
    return pl.pallas_call(
        prepare_kernel,
        in_specs=[ANY, ANY],
        out_specs=[VMEM] * 3,
        out_shape=[held((width // 2, rows))] * 2 + [held((rows, width))],
        scratch_shapes=[
            pltpu.VMEM((tiles, width // tiles, width), F32),
            pltpu.VMEM((rows, width), BF16),
            pltpu.SemaphoreType.DMA((tiles + 1,)),
        ],
        compiler_params=room(20),
    )(far(inv_gram), far(features))


def held(shape, dtype=F32):
    return pltpu.VMEM(shape, dtype)


def near(value):
    return pltpu.with_memory_space_constraint(value, pltpu.VMEM)


def far(value):
    return pltpu.with_memory_space_constraint(value, pltpu.HBM)


Z_PLACES = tuple(
    tuple((4 * slot + 2 * k + h, k, h, 2) for k in range(2) for h in range(2)) for slot in range(4)
)
X_PLACES = (
    ((0, 0, 0, 1), (1, 1, 0, 1)),
    ((2, 0, 0, 1), (3, 1, 0, 1)),
    tuple((4 + 2 * k + h, k, h, 2) for k in range(2) for h in range(2)),
    ((8, 0, 0, 1), (9, 1, 0, 1)),
)
Z_COUNT, X_COUNT = 16, 10


def fetch(slot_ref, places, refs, landing, sems):
    for slot, parts in enumerate(places):

        @pl.when(slot_ref[0] == slot)
        def _():
            for index, k, part, count in parts:
                size = landing.shape[1] // count
                target = landing.at[k, pl.ds(part * size, size)]
                pltpu.make_async_copy(refs[index], target, sems.at[k]).start()


def wait_fetch(landing, sems):
    for k in range(2):
        pltpu.make_async_copy(landing.at[k], landing.at[k], sems.at[k]).wait()


def landing_of(shape):
    return [pltpu.VMEM((2,) + shape, F32), pltpu.SemaphoreType.DMA((2,))]


def partial_sum(landing, scaled):
    half = scaled.shape[1] // 2
    total = None
    for k in range(2):
        value = landing[k]
        high = value.astype(BF16)
        low = (value - high.astype(F32)).astype(BF16)
        left = scaled[:, k * half : (k + 1) * half]
        part = dot_t(left, low) + dot_t(left, high)
        total = part if total is None else total + part
    return total


def put_pieces(out_ref, total, chunk):
    tiles = total.shape[1] // LANES
    for g in range(total.shape[0] // chunk):
        for t in range(tiles):
            out_ref[g * tiles + t, :chunk, :] = total[
                g * chunk : (g + 1) * chunk, t * LANES : (t + 1) * LANES
            ]


def take_copies(everyone_ref, groups):
    tiles = everyone_ref.shape[0] // groups
    rows = []
    for g in range(groups):
        rows.append(
            jnp.concatenate([everyone_ref[g * tiles + t] for t in range(tiles)], axis=1)
        )
    return jnp.concatenate(rows, axis=0)


def label_parts(lab, slices, width):
    group = jnp.zeros_like(lab)
    for d in range(1, slices):
        group = group + (lab >= d * width).astype(jnp.int32)
    return group, lab - group * width


def first_kernel(slices, padded, slice_ref, slot_ref, lab_ref, *refs):
    z_refs, (out_ref, landing, sems) = refs[:-3], refs[-3:]
    fetch(slot_ref, Z_PLACES, z_refs, landing, sems)
    lab = lab_ref[...]
    group, low_label = label_parts(lab, slices, C // slices)
    row = lax.broadcasted_iota(jnp.int32, (LANES, lab.shape[1]), 0)
    low_hot = jnp.where(low_label == row, 1.0, 0.0)
    onehot = jnp.where(group == slice_ref[0], low_hot, 0.0)[:padded].astype(BF16)
    group_row = lax.broadcasted_iota(jnp.int32, (slices, lab.shape[1]), 0)
    group_hot = jnp.where(group == group_row, 1.0, 0.0).astype(BF16)
    counts = dot_t(group_hot, low_hot.astype(BF16))
    chips, deep, _ = out_ref.shape
    chunk = deep - slices
    out_ref[:, chunk:, :] = jnp.broadcast_to(counts[None], (chips, slices, LANES))
    wait_fetch(landing, sems)
    put_pieces(out_ref, partial_sum(landing, onehot), chunk)


def middle_kernel(total_rows, slice_ref, part_ref, in_ref, *out_refs):
    summed = jnp.sum(in_ref[...], axis=0)
    copies_ref = out_refs[0]
    chunk = copies_ref.shape[1]
    solved = summed[:chunk]
    if len(out_refs) == 2:
        totals = summed[chunk:]
        out_refs[1][...] = totals
        row = lax.broadcasted_iota(jnp.int32, totals.shape, 0)
        mine = jnp.sum(jnp.where(row == slice_ref[0], totals, 0.0), axis=0, keepdims=True)
        scale = jnp.where(mine > 0.0, total_rows / (C * jnp.maximum(mine, 1.0)), 0.0)
        scale = scale.astype(BF16).astype(F32)
        lane = lax.broadcasted_iota(jnp.int32, (chunk, LANES), 1)
        here = lax.broadcasted_iota(jnp.int32, (chunk, LANES), 0) + part_ref[0] * chunk
        solved = solved * jnp.sum(jnp.where(lane == here, scale, 0.0), axis=1, keepdims=True)
    copies_ref[...] = jnp.broadcast_to(solved[None], copies_ref.shape)


def middle(slices, total_rows, slice_index, part_index, arrived, chunk):
    chips, deep, _ = arrived.shape
    shapes = [held((chips, chunk, LANES))]
    if deep > chunk:
        shapes.append(held((slices, LANES)))
    return pl.pallas_call(
        functools.partial(middle_kernel, total_rows),
        in_specs=[SMEM, SMEM, VMEM],
        out_specs=[VMEM] * len(shapes),
        out_shape=shapes,
        compiler_params=room(8),
    )(slice_index, part_index, near(arrived))


def update(solved, landing, residual):
    rows = landing.shape[1]
    solved = solved.astype(BF16)
    parts = [
        residual[:, k * rows : (k + 1) * rows] - dot_t(solved, landing[k].astype(BF16))
        for k in range(2)
    ]
    return jnp.concatenate(parts, axis=1)


def second_kernel(
    slices, total_rows, groups, slice_ref, x_slot_ref, z_slot_ref, lab_ref, totals_ref,
    everyone_ref, *refs,
):
    x_refs, z_refs, refs = refs[:X_COUNT], refs[X_COUNT:][:Z_COUNT], refs[X_COUNT + Z_COUNT :]
    solved_ref, residual_ref, weight_ref, out_ref, x_land, x_sems, z_land, z_sems = refs
    fetch(x_slot_ref, X_PLACES, x_refs, x_land, x_sems)
    fetch(z_slot_ref, Z_PLACES, z_refs, z_land, z_sems)
    lab = lab_ref[...]
    group, low_label = label_parts(lab, slices, C // slices)
    solved = take_copies(everyone_ref, groups)
    solved_ref[...] = solved
    padded = solved.shape[0]
    row = lax.broadcasted_iota(jnp.int32, (padded, lab.shape[1]), 0)
    hit = low_label == row
    columns = totals_ref[...].T
    spread = jnp.zeros((padded, lab.shape[1]), F32)
    for d in range(slices):
        spread = jnp.where(group == d, columns[:padded, d : d + 1], spread)
    row_count = jnp.sum(jnp.where(hit, spread, 0.0), axis=0, keepdims=True)
    weight = total_rows / (C * row_count)
    weight_ref[...] = jnp.broadcast_to(weight, weight_ref.shape)
    onehot = jnp.where(hit & (group == slice_ref[0]), 1.0, 0.0)
    wait_fetch(x_land, x_sems)
    residual = update(solved, x_land, onehot)
    residual_ref[...] = residual
    wait_fetch(z_land, z_sems)
    put_pieces(out_ref, partial_sum(z_land, (weight * residual).astype(BF16)), out_ref.shape[1])


def step_kernel(groups, x_slot_ref, z_slot_ref, everyone_ref, old_ref, weight_ref, *refs):
    x_refs, z_refs, refs = refs[:X_COUNT], refs[X_COUNT:][:Z_COUNT], refs[X_COUNT + Z_COUNT :]
    solved_ref, residual_ref, out_ref, x_land, x_sems, z_land, z_sems = refs
    fetch(x_slot_ref, X_PLACES, x_refs, x_land, x_sems)
    fetch(z_slot_ref, Z_PLACES, z_refs, z_land, z_sems)
    solved = take_copies(everyone_ref, groups)
    solved_ref[...] = solved
    wait_fetch(x_land, x_sems)
    residual = update(solved, x_land, old_ref[...])
    residual_ref[...] = residual
    scaled = (weight_ref[0:1, :] * residual).astype(BF16)
    wait_fetch(z_land, z_sems)
    put_pieces(out_ref, partial_sum(z_land, scaled), out_ref.shape[1])


def last_kernel(
    blocks, groups, width, place_ref, x_slot_ref, everyone_ref, *refs,
):
    solved_refs, refs = refs[: blocks - 1], refs[blocks - 1 :]
    rows_refs, refs = refs[: blocks - 1], refs[blocks - 1 :]
    x_refs, (out_ref, x_land, x_sems, turned) = refs[:X_COUNT], refs[X_COUNT:]
    fetch(x_slot_ref, X_PLACES, x_refs, x_land, x_sems)
    last_solved = take_copies(everyone_ref, groups)
    rows = x_land.shape[1]
    head = out_ref.shape[1] - width
    share = 2 * head
    for b in range(blocks):
        solved = last_solved if b == blocks - 1 else solved_refs[b][...]
        tile = jnp.zeros((solved.shape[0], LANES), F32)
        for t in range(solved.shape[1] // LANES):
            tile = jnp.where(place_ref[1] == t, solved[:, t * LANES : (t + 1) * LANES], tile)
        empty = jnp.zeros((LANES - tile.shape[0], LANES), F32)
        turned[...] = jnp.concatenate([tile, empty], axis=0).T
        for k in range(2):
            begin = place_ref[2] * (2 * share) + k * share
            begin = pl.multiple_of(begin, ROW_TILE)
            for h in range(2):
                out_ref[2 * b + k, :head, h * LANES : (h + 1) * LANES] = turned[
                    pl.ds(pl.multiple_of(begin + h * head, ROW_TILE), head), :
                ]
    wait_fetch(x_land, x_sems)
    last = update(last_solved, x_land, rows_refs[-1][...])
    for b in range(blocks):
        value = last if b == blocks - 1 else rows_refs[b][...]
        for k in range(2):
            mine = jnp.where(place_ref[0] == k, value[:width, :rows], value[:width, rows:])
            out_ref[2 * b + k, head:, :] = mine


def join_kernel(in_ref, weights_ref, after_ref):
    slices, deep, _ = in_ref.shape
    width = C // slices
    head = deep - width
    for d in range(slices):
        for h in range(2):
            weights_ref[h * head : (h + 1) * head, d * width : (d + 1) * width] = in_ref[
                d, :head, h * LANES : h * LANES + width
            ]
    joined = jnp.concatenate([in_ref[d, head:, :] for d in range(slices)], axis=0)
    after_ref[0] = joined.T


def shifted(value, by):
    count = lax.axis_size("feat")
    return lax.ppermute(value, "feat", [(i, (i + by) % count) for i in range(count)])


def exchange(value):
    return lax.all_to_all(value, XZ, 0, 0, tiled=True)


def halves(value):
    middle_row = value.shape[0] // 2
    return value[:middle_row], value[middle_row:]


def local(features, labels, inv_gram):
    rows_here, block_width = features.shape
    blocks = lax.axis_size("feat")
    cores = lax.axis_size("core")
    groups = lax.axis_size("x")
    depth = lax.axis_size("z")
    chips = groups * depth
    slices = blocks * cores
    width = C // slices
    tile_rows = groups * ROW_TILE
    padded = -(-width // tile_rows) * tile_rows
    chunk = padded // groups
    core = lax.axis_index("core").astype(jnp.int32)
    feat = lax.axis_index("feat").astype(jnp.int32)
    x_index = lax.axis_index("x").astype(jnp.int32)
    chip = x_index * depth + lax.axis_index("z").astype(jnp.int32)
    per_tile = LANES * chips // block_width
    place = jnp.stack([core, chip // per_tile, chip % per_tile])
    slice_index = (feat * cores + core)[None]
    part_index = x_index[None]
    total_rows = float(rows_here * chips * cores)
    both = cores * rows_here

    def slot(b):
        return lax.rem(feat + (blocks - b), blocks)[None]

    z0, z1, x_own = prepare(features, inv_gram)
    z_shape = (block_width, rows_here)
    lab = jnp.concatenate([labels, swap_cores(labels)])[None, :]

    def move(value, by):
        return shifted(value, by)

    def swap(value):
        return swap_cores(value)

    z_up0, z_down1 = move(z0, 1), move(z1, -1)
    z_up1, z_down0 = move(z1, 1), move(z0, -1)
    z_far0, z_far1 = move(z_up0, 1), move(z_down1, -1)
    x_up, x_down = move(x_own, 1), move(x_own, -1)
    z_all = [z0, z1, swap(z0), swap(z1)]
    z_all += [z_up0, z_up1, swap(z_up0), swap(z_up1)]
    z_all += [z_far0, z_far1, swap(z_far0), swap(z_far1)]
    z_all += [z_down0, z_down1, swap(z_down0), swap(z_down1)]
    z_all = [far(z) for z in z_all]
    x_far0 = move(halves(x_up)[0], 1)
    x_far1 = move(halves(x_down)[1], -1)
    x_all = [x_own, swap(x_own), x_up, swap(x_up)]
    x_all += [x_far0, x_far1, swap(x_far0), swap(x_far1)]
    x_all += [x_down, swap(x_down)]
    x_all = [far(x) for x in x_all]

    pieces = pl.pallas_call(
        functools.partial(first_kernel, slices, padded),
        in_specs=[SMEM, SMEM, VMEM] + [ANY] * Z_COUNT,
        out_specs=VMEM,
        out_shape=held((chips, chunk + slices, LANES)),
        scratch_shapes=landing_of(z_shape),
        compiler_params=room(12),
    )(slice_index, slot(0), lab, *z_all)

    rows_shape = held((padded, both))
    solved_shape = held((padded, block_width))
    pieces_shape = held((chips, chunk, LANES))
    kept_rows = []
    kept_solved = []
    totals = weight = None
    for b in range(blocks):
        arrived = exchange(pieces)
        result = middle(slices, total_rows, slice_index, part_index, arrived, chunk)
        if b == 0:
            totals = result[1]
        everyone = exchange(result[0])
        if b == 0:
            solved, residual, weight, pieces = pl.pallas_call(
                functools.partial(second_kernel, slices, total_rows, groups),
                in_specs=[SMEM] * 3 + [VMEM] * 3 + [ANY] * (X_COUNT + Z_COUNT),
                out_specs=[VMEM] * 4,
                out_shape=[solved_shape, rows_shape, held((ROW_TILE, both)), pieces_shape],
                scratch_shapes=landing_of(x_own.shape) + landing_of(z_shape),
                compiler_params=room(16),
            )(slice_index, slot(b), slot(b + 1), lab, near(totals), near(everyone),
              *x_all, *z_all)
        elif b < blocks - 1:
            solved, residual, pieces = pl.pallas_call(
                functools.partial(step_kernel, groups),
                in_specs=[SMEM] * 2 + [VMEM] * 3 + [ANY] * (X_COUNT + Z_COUNT),
                out_specs=[VMEM] * 3,
                out_shape=[solved_shape, rows_shape, pieces_shape],
                scratch_shapes=landing_of(x_own.shape) + landing_of(z_shape),
                compiler_params=room(16),
            )(slot(b), slot(b + 1), near(everyone), near(kept_rows[-1]), near(weight),
              *x_all, *z_all)
        else:
            head = block_width // (chips * cores) // 2
            sends = pl.pallas_call(
                functools.partial(last_kernel, blocks, groups, width),
                in_specs=[SMEM] * 2 + [VMEM] * (2 * blocks - 1) + [ANY] * X_COUNT,
                out_specs=VMEM,
                out_shape=held((slices, head + width, rows_here)),
                scratch_shapes=landing_of(x_own.shape) + [pltpu.VMEM((LANES, LANES), F32)],
                compiler_params=room(14),
            )(place, slot(b), *map(near, (everyone, *kept_solved, *kept_rows)), *x_all)
        if b < blocks - 1:
            kept_solved.append(solved)
            kept_rows.append(residual)

    got = near(lax.all_to_all(sends, ("feat", "core"), 0, 0, tiled=True))
    return pl.pallas_call(
        join_kernel,
        in_specs=[VMEM],
        out_specs=[VMEM, VMEM],
        out_shape=[
            jax.ShapeDtypeStruct((block_width // (chips * cores), C), F32),
            jax.ShapeDtypeStruct((1, rows_here, C), F32),
        ],
        compiler_params=room(12),
    )(got)


def solution(mesh):
    sizes = dict(mesh.shape)
    fine = Mesh(mesh.devices.reshape(sizes["feat"], 4, 8, 2), ("feat", "x", "z", "core"))
    rows = ("x", "z", "core")
    in_specs = (P(rows, "feat"), P(rows), P("feat", None, None))
    out_specs = (P(("feat",) + rows, None), P("feat", rows, None))

    return jax.shard_map(local, mesh=fine, in_specs=in_specs, out_specs=out_specs, check_vma=False)
```

```python
import functools

import jax
import jax.numpy as jnp
from jax import lax
from jax.experimental import pallas as pl
from jax.experimental.pallas import tpu as pltpu
from jax.sharding import Mesh, PartitionSpec as P


C = 640
LANES = 128
ROW_TILE = 8
XZ = ("x", "z")
F32 = jnp.float32
BF16 = jnp.bfloat16
VMEM = pl.BlockSpec(memory_space=pltpu.VMEM)
SMEM = pl.BlockSpec(memory_space=pltpu.SMEM)
ANY = pl.BlockSpec(memory_space=pl.ANY)


def room(mib):
    return pltpu.CompilerParams(vmem_limit_bytes=mib << 20)


def dot(left, right):
    return jnp.dot(left, right, preferred_element_type=F32)


def dot_t(left, right):
    return lax.dot_general(left, right, (((1,), (1,)), ((), ())), preferred_element_type=F32)


def swap_cores(value):
    return lax.ppermute(value, "core", [(0, 1), (1, 0)])


def prepare_kernel(feat_ref, gram_ref, x_ref, z_ref, early_ref, xf_ref, gram_land, x_land, sems):
    tiles, tile, _ = gram_land.shape
    x_copy = pltpu.make_async_copy(x_ref, x_land, sems.at[tiles])
    x_copy.start()
    copies = []
    for t in range(tiles):
        source = gram_ref.at[0, pl.ds(t * tile, tile)]
        copies.append(pltpu.make_async_copy(source, gram_land.at[t], sems.at[t]))
        copies[t].start()
    x_copy.wait()
    x = x_land[...]
    wide = x.astype(F32)
    xf_ref[...] = wide
    for t in range(tiles):
        copies[t].wait()
        gram = gram_land[t]
        high = gram.astype(BF16)
        rest = gram - high.astype(F32)
        mid = rest.astype(BF16)
        low = (rest - mid.astype(F32)).astype(BF16)
        z = (dot_t(x, low) + dot_t(x, mid)) + dot_t(x, high)
        at = pl.ds(t * tile, tile)
        z_ref[:, at] = z
        early_ref[:, at] = jnp.where(feat_ref[0] == 0, wide[:, t * tile : (t + 1) * tile], z)


def prepare(features, inv_gram, feat_index, tiles=4):
    rows, width = features.shape
    return pl.pallas_call(
        prepare_kernel,
        in_specs=[SMEM, ANY, ANY],
        out_specs=[VMEM] * 3,
        out_shape=[held((rows, width))] * 3,
        scratch_shapes=[
            pltpu.VMEM((tiles, width // tiles, width), F32),
            pltpu.VMEM((rows, width), BF16),
            pltpu.SemaphoreType.DMA((tiles + 1,)),
        ],
        compiler_params=room(20),
    )(feat_index, far(inv_gram), far(features))


def held(shape, dtype=F32):
    return pltpu.VMEM(shape, dtype)


def near(value):
    return pltpu.with_memory_space_constraint(value, pltpu.VMEM)


def far(value):
    return pltpu.with_memory_space_constraint(value, pltpu.HBM)


PLACES = (
    ((0, 0, 0, 1), (1, 1, 0, 1)),
    ((2, 0, 0, 1), (3, 1, 0, 1)),
    tuple((4 + 2 * k + h, k, h, 2) for k in range(2) for h in range(2)),
    ((8, 0, 0, 1), (9, 1, 0, 1)),
)
COUNT = 10


def fetch(slot_ref, refs, landing, sems):
    for slot, parts in enumerate(PLACES):

        @pl.when(slot_ref[0] == slot)
        def _():
            for index, k, part, count in parts:
                size = landing.shape[1] // count
                target = landing.at[k, pl.ds(part * size, size)]
                pltpu.make_async_copy(refs[index], target, sems.at[k]).start()


def wait_fetch(landing, sems):
    for k in range(2):
        pltpu.make_async_copy(landing.at[k], landing.at[k], sems.at[k]).wait()


def landing_of(shape):
    return [pltpu.VMEM((2,) + shape, F32), pltpu.SemaphoreType.DMA((2,))]


def partial_sum(blocks, scaled):
    half = scaled.shape[1] // 2
    total = None
    for k in range(2):
        value = blocks[k][...]
        high = value.astype(BF16)
        low = (value - high.astype(F32)).astype(BF16)
        left = scaled[:, k * half : (k + 1) * half]
        part = dot(left, low) + dot(left, high)
        total = part if total is None else total + part
    return total


def put_pieces(out_ref, total, chunk):
    tiles = total.shape[1] // LANES
    for g in range(total.shape[0] // chunk):
        for t in range(tiles):
            out_ref[g * tiles + t, :chunk, :] = total[
                g * chunk : (g + 1) * chunk, t * LANES : (t + 1) * LANES
            ]


def take_copies(everyone_ref, groups):
    tiles = everyone_ref.shape[0] // groups
    rows = []
    for g in range(groups):
        rows.append(
            jnp.concatenate([everyone_ref[g * tiles + t] for t in range(tiles)], axis=1)
        )
    return jnp.concatenate(rows, axis=0)


def label_parts(lab, slices, width):
    group = count_steps(lab, width, slices)
    return group, lab - group * width


def count_steps(value, step, steps):
    out = jnp.zeros_like(value)
    for k in range(1, steps):
        out = out + (value >= k * step).astype(jnp.int32)
    return out


def slice_class(row, groups, share):
    chunk = -(-share // ROW_TILE) * ROW_TILE
    group = count_steps(row, chunk, groups)
    inside = row - group * chunk
    return jnp.where(inside < share, group * share + inside, -1)


def first_kernel(slices, groups, core_ref, lab_ref, za_ref, zb_ref, out_ref):
    lab = lab_ref[...]
    width = C // slices
    share = width // groups
    planes = slices // 2
    group, low_label = label_parts(lab, slices, width)
    lane_row = lax.broadcasted_iota(jnp.int32, (LANES, lab.shape[1]), 0)
    low_hot = jnp.where(low_label == lane_row, 1.0, 0.0).astype(BF16)
    group_row = lax.broadcasted_iota(jnp.int32, (slices, lab.shape[1]), 0)
    group_hot = jnp.where(group == group_row, 1.0, 0.0).astype(BF16)
    counts = dot_t(group_hot, low_hot)
    chunk = planes * share
    row = lax.broadcasted_iota(jnp.int32, (groups * chunk, 1), 0)
    part = count_steps(row, chunk, groups)
    rest = row - part * chunk
    plane = count_steps(rest, share, planes)
    wanted = (2 * plane + core_ref[0]) * width + part * share + (rest - plane * share)
    onehot = jnp.where(wanted == lab, 1.0, 0.0).astype(BF16)
    out_ref[:, chunk:, :] = jnp.broadcast_to(counts[None], (out_ref.shape[0], slices, LANES))
    put_pieces(out_ref, partial_sum((za_ref, zb_ref), onehot), chunk)


def first_middle_kernel(total_rows, share, core_ref, part_ref, in_ref, out_ref, totals_ref):
    planes, _, _ = out_ref.shape
    summed = jnp.sum(in_ref[...], axis=0)
    solved = summed[: planes * share]
    totals = summed[planes * share :]
    totals_ref[...] = totals
    slice_row = lax.broadcasted_iota(jnp.int32, totals.shape, 0)
    row = lax.broadcasted_iota(jnp.int32, solved.shape, 0)
    lane = lax.broadcasted_iota(jnp.int32, solved.shape, 1)
    plane = count_steps(row, share, planes)
    counts = jnp.zeros(solved.shape, F32)
    for g in range(planes):
        mine = jnp.where(slice_row == 2 * g + core_ref[0], totals, 0.0)
        counts = jnp.where(plane == g, jnp.sum(mine, axis=0, keepdims=True), counts)
    here = part_ref[0] * share + (row - plane * share)
    counts = jnp.sum(jnp.where(lane == here, counts, 0.0), axis=1, keepdims=True)
    scale = jnp.where(counts > 0.0, total_rows / (C * jnp.maximum(counts, 1.0)), 0.0)
    solved = solved * scale.astype(BF16).astype(F32)
    out_ref[...] = jnp.zeros(out_ref.shape, F32)
    for g in range(planes):
        out_ref[g, :share, :] = solved[g * share : (g + 1) * share]


def spread_kernel(in_ref, copies_ref):
    copies_ref[...] = jnp.broadcast_to(in_ref[0][None], copies_ref.shape)


def middle_kernel(in_ref, copies_ref):
    copies_ref[...] = jnp.broadcast_to(jnp.sum(in_ref[...], axis=0)[None], copies_ref.shape)


def to_copies(kernel, arrived, shape):
    return pl.pallas_call(
        kernel,
        in_specs=[VMEM],
        out_specs=VMEM,
        out_shape=held(shape),
        compiler_params=room(8),
    )(near(arrived))


def update(solved, landing, residual):
    rows = landing.shape[1]
    solved = solved.astype(BF16)
    parts = [
        residual[:, k * rows : (k + 1) * rows] - dot_t(solved, landing[k].astype(BF16))
        for k in range(2)
    ]
    return jnp.concatenate(parts, axis=1)


def second_kernel(
    slices, total_rows, groups, slice_ref, x_slot_ref, z_slot_ref, lab_ref, totals_ref,
    everyone_ref, *refs,
):
    x_refs, z_refs, refs = refs[:COUNT], refs[COUNT:][:COUNT], refs[2 * COUNT :]
    solved_ref, residual_ref, weight_ref, out_ref, x_land, x_sems, z_land, z_sems = refs
    fetch(x_slot_ref, x_refs, x_land, x_sems)
    fetch(z_slot_ref, z_refs, z_land, z_sems)
    lab = lab_ref[...]
    group, low_label = label_parts(lab, slices, C // slices)
    solved = take_copies(everyone_ref, groups)
    solved_ref[...] = solved
    padded = solved.shape[0]
    share = C // slices // groups
    row = lax.broadcasted_iota(jnp.int32, (padded, lab.shape[1]), 0)
    hit = low_label == slice_class(row, groups, share)
    columns = totals_ref[...].T
    empty = jnp.zeros((padded // groups - share, columns.shape[1]), F32)
    columns = jnp.concatenate(
        [v for g in range(groups) for v in (columns[g * share : (g + 1) * share], empty)], axis=0
    )
    spread = jnp.zeros((padded, lab.shape[1]), F32)
    for d in range(slices):
        spread = jnp.where(group == d, columns[:, d : d + 1], spread)
    row_count = jnp.sum(jnp.where(hit, spread, 0.0), axis=0, keepdims=True)
    weight = total_rows / (C * row_count)
    weight_ref[...] = jnp.broadcast_to(weight, weight_ref.shape)
    onehot = jnp.where(hit & (group == slice_ref[0]), 1.0, 0.0)
    wait_fetch(x_land, x_sems)
    residual = update(solved, x_land, onehot)
    residual_ref[...] = residual
    wait_fetch(z_land, z_sems)
    put_pieces(out_ref, partial_sum((z_land.at[0], z_land.at[1]), (weight * residual).astype(BF16)), out_ref.shape[1])


def step_kernel(groups, x_slot_ref, z_slot_ref, everyone_ref, old_ref, weight_ref, *refs):
    x_refs, z_refs, refs = refs[:COUNT], refs[COUNT:][:COUNT], refs[2 * COUNT :]
    solved_ref, residual_ref, out_ref, x_land, x_sems, z_land, z_sems = refs
    fetch(x_slot_ref, x_refs, x_land, x_sems)
    fetch(z_slot_ref, z_refs, z_land, z_sems)
    solved = take_copies(everyone_ref, groups)
    solved_ref[...] = solved
    wait_fetch(x_land, x_sems)
    residual = update(solved, x_land, old_ref[...])
    residual_ref[...] = residual
    scaled = (weight_ref[0:1, :] * residual).astype(BF16)
    wait_fetch(z_land, z_sems)
    put_pieces(out_ref, partial_sum((z_land.at[0], z_land.at[1]), scaled), out_ref.shape[1])


def last_kernel(
    blocks, groups, width, place_ref, x_slot_ref, everyone_ref, *refs,
):
    solved_refs, refs = refs[: blocks - 1], refs[blocks - 1 :]
    rows_refs, refs = refs[: blocks - 1], refs[blocks - 1 :]
    x_refs, (out_ref, x_land, x_sems, turned) = refs[:COUNT], refs[COUNT:]
    fetch(x_slot_ref, x_refs, x_land, x_sems)
    last_solved = take_copies(everyone_ref, groups)
    rows = x_land.shape[1]
    head = out_ref.shape[1] - width
    share = 2 * head
    share_rows = width // groups
    chunk = last_solved.shape[0] // groups
    for b in range(blocks):
        solved = last_solved if b == blocks - 1 else solved_refs[b][...]
        tile = jnp.zeros((solved.shape[0], LANES), F32)
        for t in range(solved.shape[1] // LANES):
            tile = jnp.where(place_ref[1] == t, solved[:, t * LANES : (t + 1) * LANES], tile)
        empty = jnp.zeros((LANES - tile.shape[0], LANES), F32)
        turned[...] = jnp.concatenate([tile, empty], axis=0).T
        for k in range(2):
            begin = place_ref[2] * (2 * share) + k * share
            begin = pl.multiple_of(begin, ROW_TILE)
            for h in range(2):
                out_ref[2 * b + k, :head, h * LANES : (h + 1) * LANES] = turned[
                    pl.ds(pl.multiple_of(begin + h * head, ROW_TILE), head), :
                ]
    wait_fetch(x_land, x_sems)
    last = update(last_solved, x_land, rows_refs[-1][...])
    for b in range(blocks):
        value = last if b == blocks - 1 else rows_refs[b][...]
        for k in range(2):
            mine = jnp.where(place_ref[0] == k, value[:, :rows], value[:, rows:])
            for g in range(groups):
                out_ref[2 * b + k, head + g * share_rows : head + (g + 1) * share_rows, :] = mine[
                    g * chunk : g * chunk + share_rows
                ]


def join_kernel(groups, in_ref, weights_ref, after_ref):
    slices, deep, _ = in_ref.shape
    width = C // slices
    head = deep - width
    share = width // groups
    chunk = -(-share // ROW_TILE) * ROW_TILE
    for d in range(slices):
        for h in range(2):
            for g in range(groups):
                at = d * width + g * share
                come = h * LANES + g * chunk
                weights_ref[h * head : (h + 1) * head, at : at + share] = in_ref[
                    d, :head, come : come + share
                ]
    joined = jnp.concatenate([in_ref[d, head:, :] for d in range(slices)], axis=0)
    after_ref[0] = joined.T


def shifted(value, by):
    count = lax.axis_size("feat")
    return lax.ppermute(value, "feat", [(i, (i + by) % count) for i in range(count)])


def exchange(value):
    return lax.all_to_all(value, XZ, 0, 0, tiled=True)


def deal(value):
    return lax.all_to_all(value, "feat", 0, 0, tiled=True)


def halves(value):
    middle_row = value.shape[0] // 2
    return value[:middle_row], value[middle_row:]


def local(features, labels, inv_gram):
    rows_here, block_width = features.shape
    blocks = lax.axis_size("feat")
    cores = lax.axis_size("core")
    groups = lax.axis_size("x")
    depth = lax.axis_size("z")
    chips = groups * depth
    slices = blocks * cores
    width = C // slices
    share = width // groups
    chunk = -(-share // ROW_TILE) * ROW_TILE
    padded = groups * chunk
    core = lax.axis_index("core").astype(jnp.int32)
    feat = lax.axis_index("feat").astype(jnp.int32)
    x_index = lax.axis_index("x").astype(jnp.int32)
    chip = x_index * depth + lax.axis_index("z").astype(jnp.int32)
    per_tile = LANES * chips // block_width
    place = jnp.stack([core, chip // per_tile, chip % per_tile])
    slice_index = (feat * cores + core)[None]
    part_index = x_index[None]
    core_index = core[None]
    total_rows = float(rows_here * chips * cores)
    both = cores * rows_here

    def slot(b):
        return lax.rem(feat + (blocks - b), blocks)[None]

    z_own, early, late = prepare(features, inv_gram, feat[None])
    lab = jnp.concatenate([labels, swap_cores(labels)])[None, :]

    def move(value, by):
        return shifted(value, by)

    def swap(value):
        return swap_cores(value)

    def gathered(own):
        up, down = move(own, 1), move(own, -1)
        far0 = move(halves(up)[0], 1)
        far1 = move(halves(down)[1], -1)
        blocks_held = [own, swap(own), up, swap(up)]
        blocks_held += [far0, far1, swap(far0), swap(far1)]
        blocks_held += [down, swap(down)]
        return [far(block) for block in blocks_held]

    z_other = swap(z_own)
    early_all = gathered(early)
    late_all = gathered(late)
    block_shape = early.shape

    first_chunk = blocks * share
    pieces = pl.pallas_call(
        functools.partial(first_kernel, slices, groups),
        in_specs=[SMEM] + [VMEM] * 3,
        out_specs=VMEM,
        out_shape=held((chips, first_chunk + slices, LANES)),
        compiler_params=room(16),
    )(core_index, lab, near(z_own), near(z_other))

    rows_shape = held((padded, both))
    solved_shape = held((padded, block_width))
    pieces_shape = held((chips, chunk, LANES))
    kept_rows = []
    kept_solved = []
    totals = weight = None
    for b in range(blocks):
        arrived = exchange(pieces)
        if b == 0:
            parts, totals = pl.pallas_call(
                functools.partial(first_middle_kernel, total_rows, share),
                in_specs=[SMEM, SMEM, VMEM],
                out_specs=[VMEM] * 2,
                out_shape=[held((blocks, chunk, LANES)), held((slices, LANES))],
                compiler_params=room(12),
            )(core_index, part_index, near(arrived))
            parts = deal(parts)
            copies = to_copies(spread_kernel, parts, (chips, chunk, LANES))
        else:
            copies = to_copies(middle_kernel, arrived, (chips, chunk, LANES))
        everyone = exchange(copies)
        x_all = early_all if b == 0 else late_all
        if b == 0:
            solved, residual, weight, pieces = pl.pallas_call(
                functools.partial(second_kernel, slices, total_rows, groups),
                in_specs=[SMEM] * 3 + [VMEM] * 3 + [ANY] * 2 * COUNT,
                out_specs=[VMEM] * 4,
                out_shape=[solved_shape, rows_shape, held((ROW_TILE, both)), pieces_shape],
                scratch_shapes=landing_of(block_shape) * 2,
                compiler_params=room(16),
            )(slice_index, slot(b), slot(b + 1), lab, near(totals), near(everyone),
              *x_all, *early_all)
        elif b < blocks - 1:
            solved, residual, pieces = pl.pallas_call(
                functools.partial(step_kernel, groups),
                in_specs=[SMEM] * 2 + [VMEM] * 3 + [ANY] * 2 * COUNT,
                out_specs=[VMEM] * 3,
                out_shape=[solved_shape, rows_shape, pieces_shape],
                scratch_shapes=landing_of(block_shape) * 2,
                compiler_params=room(16),
            )(slot(b), slot(b + 1), near(everyone), near(kept_rows[-1]), near(weight),
              *x_all, *early_all)
        else:
            head = block_width // (chips * cores) // 2
            sends = pl.pallas_call(
                functools.partial(last_kernel, blocks, groups, width),
                in_specs=[SMEM] * 2 + [VMEM] * (2 * blocks - 1) + [ANY] * COUNT,
                out_specs=VMEM,
                out_shape=held((slices, head + width, rows_here)),
                scratch_shapes=landing_of(block_shape) + [pltpu.VMEM((LANES, LANES), F32)],
                compiler_params=room(14),
            )(place, slot(b), *map(near, (everyone, *kept_solved, *kept_rows)), *x_all)
        if b < blocks - 1:
            kept_solved.append(solved)
            kept_rows.append(residual)

    got = near(lax.all_to_all(sends, ("feat", "core"), 0, 0, tiled=True))
    return pl.pallas_call(
        functools.partial(join_kernel, groups),
        in_specs=[VMEM],
        out_specs=[VMEM, VMEM],
        out_shape=[
            jax.ShapeDtypeStruct((block_width // (chips * cores), C), F32),
            jax.ShapeDtypeStruct((1, rows_here, C), F32),
        ],
        compiler_params=room(12),
    )(got)


def solution(mesh):
    sizes = dict(mesh.shape)
    fine = Mesh(mesh.devices.reshape(sizes["feat"], 4, 8, 2), ("feat", "x", "z", "core"))
    rows = ("x", "z", "core")
    in_specs = (P(rows, "feat"), P(rows), P("feat", None, None))
    out_specs = (P(("feat",) + rows, None), P("feat", rows, None))

    return jax.shard_map(local, mesh=fine, in_specs=in_specs, out_specs=out_specs, check_vma=False)
```

```python
import functools

import jax
import jax.numpy as jnp
from jax import lax
from jax.experimental import pallas as pl
from jax.experimental.pallas import tpu as pltpu
from jax.sharding import Mesh, PartitionSpec as P


C = 640
LANES = 128
ROW_TILE = 8
XZ = ("x", "z")
F32 = jnp.float32
BF16 = jnp.bfloat16
VMEM = pl.BlockSpec(memory_space=pltpu.VMEM)
SMEM = pl.BlockSpec(memory_space=pltpu.SMEM)
ANY = pl.BlockSpec(memory_space=pl.ANY)


def room(mib):
    return pltpu.CompilerParams(vmem_limit_bytes=mib << 20)


def dot(left, right):
    return jnp.dot(left, right, preferred_element_type=F32)


def dot_t(left, right):
    return lax.dot_general(left, right, (((1,), (1,)), ((), ())), preferred_element_type=F32)


def swap_cores(value):
    return lax.ppermute(value, "core", [(0, 1), (1, 0)])


def prepare_kernel(feat_ref, gram_ref, x_ref, z_ref, early_ref, xf_ref, gram_land, x_land, sems):
    tiles, tile, _ = gram_land.shape
    x_copy = pltpu.make_async_copy(x_ref, x_land, sems.at[tiles])
    x_copy.start()
    copies = []
    for t in range(tiles):
        source = gram_ref.at[0, pl.ds(t * tile, tile)]
        copies.append(pltpu.make_async_copy(source, gram_land.at[t], sems.at[t]))
        copies[t].start()
    x_copy.wait()
    x = x_land[...]
    wide = x.astype(F32)
    xf_ref[...] = wide
    for t in range(tiles):
        copies[t].wait()
        gram = gram_land[t]
        high = gram.astype(BF16)
        rest = gram - high.astype(F32)
        mid = rest.astype(BF16)
        low = (rest - mid.astype(F32)).astype(BF16)
        z = (dot_t(x, low) + dot_t(x, mid)) + dot_t(x, high)
        at = pl.ds(t * tile, tile)
        z_ref[:, at] = z
        early_ref[:, at] = jnp.where(feat_ref[0] == 0, wide[:, t * tile : (t + 1) * tile], z)


def prepare(features, inv_gram, feat_index, tiles=4):
    rows, width = features.shape
    return pl.pallas_call(
        prepare_kernel,
        in_specs=[SMEM, ANY, ANY],
        out_specs=[VMEM] * 3,
        out_shape=[held((rows, width))] * 3,
        scratch_shapes=[
            pltpu.VMEM((tiles, width // tiles, width), F32),
            pltpu.VMEM((rows, width), BF16),
            pltpu.SemaphoreType.DMA((tiles + 1,)),
        ],
        compiler_params=room(20),
    )(feat_index, far(inv_gram), far(features))


def held(shape, dtype=F32):
    return pltpu.VMEM(shape, dtype)


def near(value):
    return pltpu.with_memory_space_constraint(value, pltpu.VMEM)


def far(value):
    return pltpu.with_memory_space_constraint(value, pltpu.HBM)


PLACES = (
    ((0, 0, 0, 1), (1, 1, 0, 1)),
    ((2, 0, 0, 1), (3, 1, 0, 1)),
    tuple((4 + 2 * k + h, k, h, 2) for k in range(2) for h in range(2)),
    ((8, 0, 0, 1), (9, 1, 0, 1)),
)
COUNT = 10


def fetch(slot_ref, refs, landing, sems):
    for slot, parts in enumerate(PLACES):

        @pl.when(slot_ref[0] == slot)
        def _():
            for index, k, part, count in parts:
                size = landing.shape[1] // count
                target = landing.at[k, pl.ds(part * size, size)]
                pltpu.make_async_copy(refs[index], target, sems.at[k]).start()


def wait_fetch(landing, sems):
    for k in range(2):
        pltpu.make_async_copy(landing.at[k], landing.at[k], sems.at[k]).wait()


def landing_of(shape):
    return [pltpu.VMEM((2,) + shape, F32), pltpu.SemaphoreType.DMA((2,))]


def partial_sum(blocks, scaled):
    half = scaled.shape[1] // 2
    total = None
    for k in range(2):
        value = blocks[k][...]
        high = value.astype(BF16)
        low = (value - high.astype(F32)).astype(BF16)
        left = scaled[:, k * half : (k + 1) * half]
        part = dot(left, low) + dot(left, high)
        total = part if total is None else total + part
    return total


def put_pieces(out_ref, total, chunk):
    tiles = total.shape[1] // LANES
    for g in range(total.shape[0] // chunk):
        for t in range(tiles):
            out_ref[g * tiles + t, :chunk, :] = total[
                g * chunk : (g + 1) * chunk, t * LANES : (t + 1) * LANES
            ]


def take_copies(everyone_ref, groups):
    tiles = everyone_ref.shape[0] // groups
    rows = []
    for g in range(groups):
        rows.append(
            jnp.concatenate([everyone_ref[g * tiles + t] for t in range(tiles)], axis=1)
        )
    return jnp.concatenate(rows, axis=0)


def label_parts(lab, slices, width):
    group = count_steps(lab, width, slices)
    return group, lab - group * width


def count_steps(value, step, steps):
    out = jnp.zeros_like(value)
    for k in range(1, steps):
        out = out + (value >= k * step).astype(jnp.int32)
    return out


def slice_class(row, groups, share):
    chunk = -(-share // ROW_TILE) * ROW_TILE
    group = count_steps(row, chunk, groups)
    inside = row - group * chunk
    return jnp.where(inside < share, group * share + inside, -1)


def first_kernel(slices, groups, core_ref, lab_ref, za_ref, zb_ref, counts_ref, *out_refs):
    lab = lab_ref[...]
    width = C // slices
    group, low_label = label_parts(lab, slices, width)
    lane_row = lax.broadcasted_iota(jnp.int32, (LANES, lab.shape[1]), 0)
    low_hot = jnp.where(low_label == lane_row, 1.0, 0.0).astype(BF16)
    group_row = lax.broadcasted_iota(jnp.int32, (slices, lab.shape[1]), 0)
    group_hot = jnp.where(group == group_row, 1.0, 0.0).astype(BF16)
    counts_ref[...] = dot_t(group_hot, low_hot)
    chunk = out_refs[0].shape[1]
    padded = chunk * groups
    planes = len(out_refs)
    row = lax.broadcasted_iota(jnp.int32, (planes * padded, 1), 0)
    plane = count_steps(row, padded, planes)
    low = slice_class(row - plane * padded, groups, width // groups)
    wanted = jnp.where(low >= 0, (2 * plane + core_ref[0]) * width + low, -1)
    onehot = jnp.where(wanted == lab, 1.0, 0.0).astype(BF16)
    total = partial_sum((za_ref, zb_ref), onehot)
    for g in range(planes):
        put_pieces(out_refs[g], total[g * padded : (g + 1) * padded], chunk)


def dealt_kernel(feat_ref, counts_ref, *refs):
    dealt_refs, out_ref = refs[:-1], refs[-1]
    chips, deep, _ = out_ref.shape
    chunk = dealt_refs[0].shape[1]
    for g, dealt_ref in enumerate(dealt_refs):

        @pl.when(feat_ref[0] == g)
        def _():
            out_ref[:, :chunk, :] = dealt_ref[...]

    out_ref[:, chunk:, :] = jnp.broadcast_to(counts_ref[...][None], (chips, deep - chunk, LANES))


def first_middle_kernel(total_rows, share, slice_ref, part_ref, in_ref, copies_ref, totals_ref):
    chunk = copies_ref.shape[1]
    summed = jnp.sum(in_ref[...], axis=0)
    solved = summed[:chunk]
    totals = summed[chunk:]
    totals_ref[...] = totals
    slice_row = lax.broadcasted_iota(jnp.int32, totals.shape, 0)
    mine = jnp.sum(jnp.where(slice_row == slice_ref[0], totals, 0.0), axis=0, keepdims=True)
    scale = jnp.where(mine > 0.0, total_rows / (C * jnp.maximum(mine, 1.0)), 0.0)
    scale = scale.astype(BF16).astype(F32)
    row = lax.broadcasted_iota(jnp.int32, solved.shape, 0)
    lane = lax.broadcasted_iota(jnp.int32, solved.shape, 1)
    here = jnp.where(row < share, part_ref[0] * share + row, -1)
    solved = solved * jnp.sum(jnp.where(lane == here, scale, 0.0), axis=1, keepdims=True)
    copies_ref[...] = jnp.broadcast_to(solved[None], copies_ref.shape)


def middle_kernel(in_ref, copies_ref):
    copies_ref[...] = jnp.broadcast_to(jnp.sum(in_ref[...], axis=0)[None], copies_ref.shape)


def to_copies(kernel, arrived, shape):
    return pl.pallas_call(
        kernel,
        in_specs=[VMEM],
        out_specs=VMEM,
        out_shape=held(shape),
        compiler_params=room(8),
    )(near(arrived))


def update(solved, landing, residual):
    rows = landing.shape[1]
    solved = solved.astype(BF16)
    parts = [
        residual[:, k * rows : (k + 1) * rows] - dot_t(solved, landing[k].astype(BF16))
        for k in range(2)
    ]
    return jnp.concatenate(parts, axis=1)


def second_kernel(
    slices, total_rows, groups, slice_ref, x_slot_ref, z_slot_ref, lab_ref, totals_ref,
    everyone_ref, *refs,
):
    x_refs, z_refs, refs = refs[:COUNT], refs[COUNT:][:COUNT], refs[2 * COUNT :]
    solved_ref, residual_ref, weight_ref, out_ref, x_land, x_sems, z_land, z_sems = refs
    fetch(x_slot_ref, x_refs, x_land, x_sems)
    fetch(z_slot_ref, z_refs, z_land, z_sems)
    lab = lab_ref[...]
    group, low_label = label_parts(lab, slices, C // slices)
    solved = take_copies(everyone_ref, groups)
    solved_ref[...] = solved
    padded = solved.shape[0]
    share = C // slices // groups
    row = lax.broadcasted_iota(jnp.int32, (padded, lab.shape[1]), 0)
    hit = low_label == slice_class(row, groups, share)
    columns = totals_ref[...].T
    empty = jnp.zeros((padded // groups - share, columns.shape[1]), F32)
    columns = jnp.concatenate(
        [v for g in range(groups) for v in (columns[g * share : (g + 1) * share], empty)], axis=0
    )
    spread = jnp.zeros((padded, lab.shape[1]), F32)
    for d in range(slices):
        spread = jnp.where(group == d, columns[:, d : d + 1], spread)
    row_count = jnp.sum(jnp.where(hit, spread, 0.0), axis=0, keepdims=True)
    weight = total_rows / (C * row_count)
    weight_ref[...] = jnp.broadcast_to(weight, weight_ref.shape)
    onehot = jnp.where(hit & (group == slice_ref[0]), 1.0, 0.0)
    wait_fetch(x_land, x_sems)
    residual = update(solved, x_land, onehot)
    residual_ref[...] = residual
    wait_fetch(z_land, z_sems)
    put_pieces(out_ref, partial_sum((z_land.at[0], z_land.at[1]), (weight * residual).astype(BF16)), out_ref.shape[1])


def step_kernel(groups, x_slot_ref, z_slot_ref, everyone_ref, old_ref, weight_ref, *refs):
    x_refs, z_refs, refs = refs[:COUNT], refs[COUNT:][:COUNT], refs[2 * COUNT :]
    solved_ref, residual_ref, out_ref, x_land, x_sems, z_land, z_sems = refs
    fetch(x_slot_ref, x_refs, x_land, x_sems)
    fetch(z_slot_ref, z_refs, z_land, z_sems)
    solved = take_copies(everyone_ref, groups)
    solved_ref[...] = solved
    wait_fetch(x_land, x_sems)
    residual = update(solved, x_land, old_ref[...])
    residual_ref[...] = residual
    scaled = (weight_ref[0:1, :] * residual).astype(BF16)
    wait_fetch(z_land, z_sems)
    put_pieces(out_ref, partial_sum((z_land.at[0], z_land.at[1]), scaled), out_ref.shape[1])


def last_kernel(
    blocks, groups, width, place_ref, x_slot_ref, everyone_ref, *refs,
):
    solved_refs, refs = refs[: blocks - 1], refs[blocks - 1 :]
    rows_refs, refs = refs[: blocks - 1], refs[blocks - 1 :]
    x_refs, (out_ref, x_land, x_sems, turned) = refs[:COUNT], refs[COUNT:]
    fetch(x_slot_ref, x_refs, x_land, x_sems)
    last_solved = take_copies(everyone_ref, groups)
    rows = x_land.shape[1]
    head = out_ref.shape[1] - width
    share = 2 * head
    share_rows = width // groups
    chunk = last_solved.shape[0] // groups
    for b in range(blocks):
        solved = last_solved if b == blocks - 1 else solved_refs[b][...]
        tile = jnp.zeros((solved.shape[0], LANES), F32)
        for t in range(solved.shape[1] // LANES):
            tile = jnp.where(place_ref[1] == t, solved[:, t * LANES : (t + 1) * LANES], tile)
        empty = jnp.zeros((LANES - tile.shape[0], LANES), F32)
        turned[...] = jnp.concatenate([tile, empty], axis=0).T
        for k in range(2):
            begin = place_ref[2] * (2 * share) + k * share
            begin = pl.multiple_of(begin, ROW_TILE)
            for h in range(2):
                out_ref[2 * b + k, :head, h * LANES : (h + 1) * LANES] = turned[
                    pl.ds(pl.multiple_of(begin + h * head, ROW_TILE), head), :
                ]
    wait_fetch(x_land, x_sems)
    last = update(last_solved, x_land, rows_refs[-1][...])
    for b in range(blocks):
        value = last if b == blocks - 1 else rows_refs[b][...]
        for k in range(2):
            mine = jnp.where(place_ref[0] == k, value[:, :rows], value[:, rows:])
            for g in range(groups):
                out_ref[2 * b + k, head + g * share_rows : head + (g + 1) * share_rows, :] = mine[
                    g * chunk : g * chunk + share_rows
                ]


def join_kernel(groups, in_ref, weights_ref, after_ref):
    slices, deep, _ = in_ref.shape
    width = C // slices
    head = deep - width
    share = width // groups
    chunk = -(-share // ROW_TILE) * ROW_TILE
    for d in range(slices):
        for h in range(2):
            for g in range(groups):
                at = d * width + g * share
                come = h * LANES + g * chunk
                weights_ref[h * head : (h + 1) * head, at : at + share] = in_ref[
                    d, :head, come : come + share
                ]
    joined = jnp.concatenate([in_ref[d, head:, :] for d in range(slices)], axis=0)
    after_ref[0] = joined.T


def shifted(value, by):
    count = lax.axis_size("feat")
    return lax.ppermute(value, "feat", [(i, (i + by) % count) for i in range(count)])


def exchange(value):
    return lax.all_to_all(value, XZ, 0, 0, tiled=True)


def halves(value):
    middle_row = value.shape[0] // 2
    return value[:middle_row], value[middle_row:]


def local(features, labels, inv_gram):
    rows_here, block_width = features.shape
    blocks = lax.axis_size("feat")
    cores = lax.axis_size("core")
    groups = lax.axis_size("x")
    depth = lax.axis_size("z")
    chips = groups * depth
    slices = blocks * cores
    width = C // slices
    share = width // groups
    chunk = -(-share // ROW_TILE) * ROW_TILE
    padded = groups * chunk
    core = lax.axis_index("core").astype(jnp.int32)
    feat = lax.axis_index("feat").astype(jnp.int32)
    x_index = lax.axis_index("x").astype(jnp.int32)
    chip = x_index * depth + lax.axis_index("z").astype(jnp.int32)
    per_tile = LANES * chips // block_width
    place = jnp.stack([core, chip // per_tile, chip % per_tile])
    slice_index = (feat * cores + core)[None]
    part_index = x_index[None]
    core_index = core[None]
    total_rows = float(rows_here * chips * cores)
    both = cores * rows_here

    def slot(b):
        return lax.rem(feat + (blocks - b), blocks)[None]

    z_own, early, late = prepare(features, inv_gram, feat[None])
    lab = jnp.concatenate([labels, swap_cores(labels)])[None, :]

    def move(value, by):
        return shifted(value, by)

    def swap(value):
        return swap_cores(value)

    def gathered(own):
        up, down = move(own, 1), move(own, -1)
        far0 = move(halves(up)[0], 1)
        far1 = move(halves(down)[1], -1)
        blocks_held = [own, swap(own), up, swap(up)]
        blocks_held += [far0, far1, swap(far0), swap(far1)]
        blocks_held += [down, swap(down)]
        return [far(block) for block in blocks_held]

    z_other = swap(z_own)
    early_all = gathered(early)
    late_all = gathered(late)
    block_shape = early.shape

    counts, *dealt = pl.pallas_call(
        functools.partial(first_kernel, slices, groups),
        in_specs=[SMEM] + [VMEM] * 3,
        out_specs=[VMEM] * (1 + blocks),
        out_shape=[held((slices, LANES))] + [held((chips, chunk, LANES))] * blocks,
        compiler_params=room(16),
    )(core_index, lab, near(z_own), near(z_other))
    for g in range(1, blocks):
        dealt[g] = lax.ppermute(dealt[g], "feat", [(0, g)])
    pieces = pl.pallas_call(
        dealt_kernel,
        in_specs=[SMEM] + [VMEM] * (1 + blocks),
        out_specs=VMEM,
        out_shape=held((chips, chunk + slices, LANES)),
        compiler_params=room(8),
    )(feat[None], *map(near, (counts, *dealt)))

    rows_shape = held((padded, both))
    solved_shape = held((padded, block_width))
    pieces_shape = held((chips, chunk, LANES))
    kept_rows = []
    kept_solved = []
    totals = weight = None
    for b in range(blocks):
        arrived = exchange(pieces)
        if b == 0:
            copies, totals = pl.pallas_call(
                functools.partial(first_middle_kernel, total_rows, share),
                in_specs=[SMEM, SMEM, VMEM],
                out_specs=[VMEM] * 2,
                out_shape=[held((chips, chunk, LANES)), held((slices, LANES))],
                compiler_params=room(8),
            )(slice_index, part_index, near(arrived))
        else:
            copies = to_copies(middle_kernel, arrived, (chips, chunk, LANES))
        everyone = exchange(copies)
        x_all = early_all if b == 0 else late_all
        if b == 0:
            solved, residual, weight, pieces = pl.pallas_call(
                functools.partial(second_kernel, slices, total_rows, groups),
                in_specs=[SMEM] * 3 + [VMEM] * 3 + [ANY] * 2 * COUNT,
                out_specs=[VMEM] * 4,
                out_shape=[solved_shape, rows_shape, held((ROW_TILE, both)), pieces_shape],
                scratch_shapes=landing_of(block_shape) * 2,
                compiler_params=room(16),
            )(slice_index, slot(b), slot(b + 1), lab, near(totals), near(everyone),
              *x_all, *early_all)
        elif b < blocks - 1:
            solved, residual, pieces = pl.pallas_call(
                functools.partial(step_kernel, groups),
                in_specs=[SMEM] * 2 + [VMEM] * 3 + [ANY] * 2 * COUNT,
                out_specs=[VMEM] * 3,
                out_shape=[solved_shape, rows_shape, pieces_shape],
                scratch_shapes=landing_of(block_shape) * 2,
                compiler_params=room(16),
            )(slot(b), slot(b + 1), near(everyone), near(kept_rows[-1]), near(weight),
              *x_all, *early_all)
        else:
            head = block_width // (chips * cores) // 2
            sends = pl.pallas_call(
                functools.partial(last_kernel, blocks, groups, width),
                in_specs=[SMEM] * 2 + [VMEM] * (2 * blocks - 1) + [ANY] * COUNT,
                out_specs=VMEM,
                out_shape=held((slices, head + width, rows_here)),
                scratch_shapes=landing_of(block_shape) + [pltpu.VMEM((LANES, LANES), F32)],
                compiler_params=room(14),
            )(place, slot(b), *map(near, (everyone, *kept_solved, *kept_rows)), *x_all)
        if b < blocks - 1:
            kept_solved.append(solved)
            kept_rows.append(residual)

    got = near(lax.all_to_all(sends, ("feat", "core"), 0, 0, tiled=True))
    return pl.pallas_call(
        functools.partial(join_kernel, groups),
        in_specs=[VMEM],
        out_specs=[VMEM, VMEM],
        out_shape=[
            jax.ShapeDtypeStruct((block_width // (chips * cores), C), F32),
            jax.ShapeDtypeStruct((1, rows_here, C), F32),
        ],
        compiler_params=room(12),
    )(got)


def solution(mesh):
    sizes = dict(mesh.shape)
    fine = Mesh(mesh.devices.reshape(sizes["feat"], 4, 8, 2), ("feat", "x", "z", "core"))
    rows = ("x", "z", "core")
    in_specs = (P(rows, "feat"), P(rows), P("feat", None, None))
    out_specs = (P(("feat",) + rows, None), P("feat", rows, None))

    return jax.shard_map(local, mesh=fine, in_specs=in_specs, out_specs=out_specs, check_vma=False)
```
